32 devices in a mesh: groups: 2 (over x), blk: 16 (over z, y, core).
Axes of the slice: x: 2, y: 2, z: 4, core: 2. Of those that a mesh axis runs over, the one named last changes fastest.
Arguments:
- hidden: bfloat16 [16384, 2048], P(('groups', 'blk')), parts along dimension 0, may hold values from -6 to 6
- kept_idx: int32 [32, 128], P(('groups', 'blk')), parts along dimension 0, may hold values from 0 to 511, as said below
- kept_count: int32 [32], P(('groups', 'blk')), parts along dimension 0, may hold values from 0 to 128, as said below
- router: bfloat16 [2048], replicated, may hold values from -0.125 to 0.125
- norm_gain: float32 [2048], replicated, may hold values from 0.25 to 1.75
- qk_gain: float32 [2, 64], replicated, may hold values from 1 to 7
- query_weight: bfloat16 [2048, 2048], P('blk'), may hold values from -1 to 1
- key_weight: bfloat16 [2048, 128], P('blk'), may hold values from -1 to 1
- value_weight: bfloat16 [2048, 128], P('blk'), may hold values from -0.125 to 0.125
- out_weight: bfloat16 [2048, 2048], P('blk'), may hold values from -0.375 to 0.375
Outputs:
- mixed: bfloat16 [16384, 2048], P(('groups', 'blk')), parts along dimension 0
The draws below stay inside these ranges and needn't reach their ends.
There are 2 independent parts, one for each index of `groups`. The reference program is written for one: setup_inputs(seed, part) draws one part's arguments, and reference() takes and returns one part's arrays. A program takes and returns all parts, laid end to end along the dimension named above; an argument that names none is the same for every part. Nothing has to cross between parts.
Inputs may be any that keep to these rules, and one draw needn't show every extreme that they name: `kept_count`: the counts sum to 1024; in every draw some shard's count is exactly 128. `kept_idx`: in row s the first kept_count[s] entries are distinct local token indices in increasing order; entries past the count are 0.
All inputs are finite; a program needn't handle non-finite values.
Results may differ from the reference program's by a relative error of at most 0.01.
Values may be sent and summed in bfloat16 or wider, within the bound.
A program may use at most 128 MiB of HBM per device.

```python
import math
import jax
import jax.numpy as jnp
from jax import lax

D = 2048
Q_HEADS = 32
KV_HEADS = 2
HEAD = 64
TOK_DEV = 512
KEEP_DEV = 64
CAP = 128
KEEP = 1024
TOKENS = 8192
N_BLK = 16


def lists_draw(key):
    base_key = jax.random.fold_in(key, 7)
    order_key, shift_key, rows_key = jax.random.split(base_key, 3)
    shard_order = jax.random.permutation(order_key, N_BLK)
    pair_total = N_BLK // 2
    shifts = jax.random.randint(shift_key, (pair_total,), 0, KEEP_DEV + 1)
    shifts = shifts.at[0].set(KEEP_DEV)
    pair_counts = jnp.concatenate([KEEP_DEV + shifts, KEEP_DEV - shifts]).astype(jnp.int32)
    counts = jnp.zeros((N_BLK,), jnp.int32).at[shard_order].set(pair_counts)
    row_keys = jax.random.split(rows_key, N_BLK)

    def one_shard(sub_key, kept_total):
        shuffled = jax.random.permutation(sub_key, TOK_DEV)
        placement = jnp.argsort(shuffled, stable=True)
        chosen = placement < kept_total
        slot_index = jnp.cumsum(chosen.astype(jnp.int32)) - 1
        target = jnp.where(chosen, slot_index, CAP)
        return jnp.zeros((CAP,), jnp.int32).at[target].set(jnp.arange(TOK_DEV, dtype=jnp.int32), mode='drop')
    lists = jax.vmap(one_shard)(row_keys, counts)
    return (counts, lists)


def draw_kept_count(key, part):
    return lists_draw(key)[0]


def draw_kept_idx(key, part):
    return lists_draw(key)[1]


def projection_pair(key):
    base_key = jax.random.fold_in(key, 11)
    key_part, query_part = jax.random.split(base_key, 2)
    group_size = Q_HEADS // KV_HEADS
    key_cols = jax.random.uniform(key_part, (D, KV_HEADS, HEAD), jnp.float32, -1.0, 1.0)
    fresh = jax.random.uniform(query_part, (D, KV_HEADS, group_size, HEAD), jnp.float32, -1.0, 1.0)
    query_cols = fresh
    return (query_cols.reshape(D, Q_HEADS * HEAD), key_cols.reshape(D, KV_HEADS * HEAD))


def draw_query_weight(key, part):
    return projection_pair(key)[0].astype(jnp.bfloat16)


def draw_key_weight(key, part):
    return projection_pair(key)[1].astype(jnp.bfloat16)


def draw_qk_gain(key, part):
    base_key = jax.random.fold_in(key, 23)
    return jax.random.uniform(base_key, (2, HEAD), jnp.float32, 1.0, 2.0)


def block_levels(rng, dims, cuts, smallest, high):
    def one(dim, shards_of):
        draws = jax.random.uniform(jax.random.fold_in(jax.random.fold_in(rng, 6), dim), (shards_of,), jnp.float32, smallest / len(cuts), high / len(cuts))
        return jnp.repeat(jnp.exp(draws), dims[dim] // shards_of).reshape((-1,) + (1,) * (len(dims) - dim - 1))

    loudness = one(*cuts[0])
    for cut in cuts[1:]:
        loudness = loudness * one(*cut)
    return loudness


def noise(own_key, dims, width, most, shards=(), kind=jnp.bfloat16):
    values = width * jax.random.normal(own_key, dims, jnp.float32)
    if shards:
        values = values * block_levels(own_key, dims, shards, -0.22, 0.18)
    return jnp.clip(values, -most, most).astype(kind)


def setup_inputs(seed: int = 0, part: int = 0) -> dict:
    streams_of = jax.random.split(jax.random.key(seed), 11)
    part_keys = jax.random.split(jax.random.fold_in(streams_of[10], part), 11)
    return {
        "hidden": noise(part_keys[0], (TOKENS, D), 1.0, 6.0, ((0, 16),)),
        "kept_idx": draw_kept_idx(jax.random.fold_in(jax.random.fold_in(streams_of[10], part), 71), part),
        "kept_count": draw_kept_count(jax.random.fold_in(jax.random.fold_in(streams_of[10], part), 71), part),
        "router": noise(streams_of[3], (D,), D ** -0.5, 0.125),
        "norm_gain": jnp.clip(1.0 + 0.15 * jax.random.normal(streams_of[4], (D,), jnp.float32), 0.25, 1.75),
        "qk_gain": draw_qk_gain(jax.random.fold_in(streams_of[10], 71), part),
        "query_weight": draw_query_weight(jax.random.fold_in(streams_of[10], 71), part),
        "key_weight": draw_key_weight(jax.random.fold_in(streams_of[10], 71), part),
        "value_weight": noise(streams_of[8], (D, KV_HEADS * HEAD), D ** -0.5, 0.125, ((0, 16),)),
        "out_weight": noise(streams_of[9], (Q_HEADS * HEAD, D), (HEAD * 4) ** -0.5, 0.375, ((0, 16),)),
    }


norm_eps = 1e-06
rope_base = 1000000.0

def rms_scale(values, scales):
    return values * lax.rsqrt(lax.optimization_barrier(jnp.mean(values * values, axis=-1, keepdims=True)) + norm_eps) * scales

def rotate(values, angles):
    half_size = values.shape[-1] // 2
    lower_half = values[..., :half_size]
    upper_half = values[..., half_size:]
    cosine = jnp.cos(angles)
    sine_part = jnp.sin(angles)
    return jnp.concatenate([lower_half * cosine - upper_half * sine_part, upper_half * cosine + lower_half * sine_part], axis=-1)

def prepare(query_lin, key_lin, value_lin, qk_gain, positions):
    count_rows = positions.shape[0]
    half_size = HEAD // 2
    rotation_rates = rope_base ** (-(jnp.arange(half_size, dtype=jnp.float32) * 2.0 / HEAD))
    angles = (positions.astype(jnp.float32)[:, None] * rotation_rates[None, :])[:, None, :]
    query_heads = rms_scale(query_lin.reshape(count_rows, Q_HEADS, HEAD), qk_gain[0])
    key_heads = rms_scale(key_lin.reshape(count_rows, KV_HEADS, HEAD), qk_gain[1])
    query_heads = rotate(query_heads, angles).astype(jnp.bfloat16)
    key_heads = rotate(key_heads, angles).astype(jnp.bfloat16)
    value_heads = value_lin.reshape(count_rows, KV_HEADS, HEAD).astype(jnp.bfloat16)
    query_heads = query_heads.reshape(count_rows, KV_HEADS, Q_HEADS // KV_HEADS, HEAD)
    return (query_heads, key_heads, value_heads)

def reference(hidden, kept_idx, kept_count, router, norm_gain, qk_gain, query_weight, key_weight, value_weight, out_weight):
    starts = jnp.cumsum(kept_count) - kept_count
    slot_ids = jnp.arange(CAP, dtype=jnp.int32)
    is_valid = slot_ids[None, :] < kept_count[:, None]
    rank_grid = jnp.where(is_valid, starts[:, None] + slot_ids[None, :], KEEP).astype(jnp.int32)
    positions = (jnp.arange(N_BLK, dtype=jnp.int32)[:, None] * TOK_DEV + kept_idx).astype(jnp.int32)
    by_rank = jnp.zeros((KEEP,), jnp.int32).at[rank_grid.reshape(-1)].set(positions.reshape(-1), mode='drop')
    token_rows = hidden[by_rank]
    gate_value = jax.nn.sigmoid(jnp.dot(token_rows, router, preferred_element_type=jnp.float32))
    normed = rms_scale(token_rows.astype(jnp.float32), norm_gain).astype(jnp.bfloat16)
    query_lin = jnp.dot(normed, query_weight, preferred_element_type=jnp.float32)
    key_lin = jnp.dot(normed, key_weight, preferred_element_type=jnp.float32)
    value_lin = jnp.dot(normed, value_weight, preferred_element_type=jnp.float32)
    query_heads, key_heads, value_heads = prepare(query_lin, key_lin, value_lin, qk_gain, by_rank)
    keys_wide = key_heads.astype(jnp.float32)
    values_wide = value_heads.astype(jnp.float32)
    block_rows = math.gcd(KEEP, 256)
    all_ranks = jnp.arange(KEEP, dtype=jnp.int32)
    score_scale = 1.0 / math.sqrt(HEAD)

    def one_block(block_start):
        query_block = lax.dynamic_slice_in_dim(query_heads, block_start, block_rows, 0).astype(jnp.float32)
        scores = jnp.einsum('agch,bgh->gcab', query_block, keys_wide) * score_scale
        query_ranks = block_start + jnp.arange(block_rows, dtype=jnp.int32)
        allowed = all_ranks[None, :] <= query_ranks[:, None]
        masked = jnp.where(allowed, scores, -1e+30)
        row_top = lax.optimization_barrier(jnp.max(masked, axis=-1, keepdims=True))
        weights = jnp.where(allowed, jnp.exp(masked - row_top), 0.0)
        denominator = lax.optimization_barrier(jnp.sum(weights, axis=-1))
        rounded = lax.optimization_barrier(weights.astype(jnp.bfloat16)).astype(jnp.float32)
        mixture = jnp.einsum('gcab,bgh->gcah', rounded, values_wide) / denominator[..., None]
        return mixture.transpose(2, 0, 1, 3).reshape(block_rows, Q_HEADS * HEAD).astype(jnp.bfloat16)
    block_starts = (jnp.arange(KEEP // block_rows, dtype=jnp.int32) * block_rows).astype(jnp.int32)
    attended = lax.map(one_block, block_starts).reshape(KEEP, Q_HEADS * HEAD)
    update = jnp.dot(attended, out_weight, preferred_element_type=jnp.float32).astype(jnp.bfloat16)
    final = (token_rows.astype(jnp.float32) + gate_value[:, None] * update.astype(jnp.float32)).astype(jnp.bfloat16)
    return hidden.at[by_rank].set(final)
```

```python
import functools
import math

import jax
import jax.numpy as jnp
import numpy as np
from jax import lax
from jax.experimental import pallas as pl
from jax.experimental.pallas import tpu as pltpu
from jax.sharding import PartitionSpec as P

Q_HEADS = 32
KV_HEADS = 2
HEAD = 64
TOK_DEV = 512
KEEP_DEV = 64
CAP = 128
MESH = pl.DeviceIdType.MESH
VM = pl.BlockSpec(memory_space=pltpu.VMEM)


norm_eps = 1e-06
rope_base = 1000000.0


def rms_scale(values, scales):
    return values * lax.rsqrt(jnp.mean(values * values, axis=-1, keepdims=True) + norm_eps) * scales


def rotate(values, angles):
    half_size = values.shape[-1] // 2
    lower_half = values[..., :half_size]
    upper_half = values[..., half_size:]
    cosine = jnp.cos(angles)
    sine_part = jnp.sin(angles)
    return jnp.concatenate(
        [
            lower_half * cosine - upper_half * sine_part,
            upper_half * cosine + lower_half * sine_part,
        ],
        axis=-1,
    )


class Ring:
    def __init__(self, n):
        self.chips = n // 2
        self.arm = self.chips // 2
        self.me = lax.axis_index("blk")
        self.group = lax.axis_index("groups")
        self.chip, self.core = self.me // 2, self.me % 2
        side, row = self.chip % 2, self.chip // 2
        self.place = row * (1 - side) + (self.chips - 1 - row) * side
        self.partner = self.chip * 2 + 1 - self.core
        self.ahead = self.chip_at(self.place + 1) * 2 + self.core
        self.behind = self.chip_at(self.place - 1) * 2 + self.core

    def chip_at(self, position):
        q = lax.rem(position + 2 * self.chips, self.chips)
        far = q // self.arm
        return 2 * (q * (1 - far) + (self.chips - 1 - q) * far) + far


class Spread:
    def __init__(self, ring, own, buf, rows, sems, dup_sems=None, flip=False):
        self.ring, self.own, self.buf, self.rows, self.flip = ring, own, buf, rows, flip
        self.send, self.recv = sems
        self.dup_sems = dup_sems
        far = ring.chips // 2
        self.hops = {1: far - 1 if flip else far, -1: far if flip else far - 1}

    @staticmethod
    def semaphores(chips, count):
        return [pltpu.SemaphoreType.DMA((count, 2, chips // 2)) for _ in range(2)]

    def at(self, distance, sign, core):
        chip = self.ring.chip_at(self.ring.place - sign * distance)
        block = chip if self.dup_sems is None else chip * 2 + core
        return self.buf.at[pl.ds(pl.multiple_of(block * self.rows, self.rows), self.rows)]

    def copy(self, distance, sign, arriving):
        ring = self.ring
        place = self.at(distance if arriving else distance - 1, sign, ring.core)
        source = self.own if distance == 1 and not arriving else place
        k = 0 if sign > 0 else 1
        return pltpu.make_async_remote_copy(
            src_ref=source,
            dst_ref=place,
            send_sem=self.send.at[k, distance - 1],
            recv_sem=self.recv.at[k, distance - 1],
            device_id={"blk": ring.ahead if sign > 0 else ring.behind},
            device_id_type=MESH,
        )

    def dup(self, distance, sign, arriving=False):
        ring = self.ring
        core = 1 - ring.core if arriving else ring.core
        place = self.at(distance, sign, core)
        slot = distance if sign > 0 else self.hops[1] + distance
        source = self.own if distance == 0 and not arriving else place
        return pltpu.make_async_remote_copy(
            src_ref=source,
            dst_ref=place,
            send_sem=self.dup_sems[0].at[slot],
            recv_sem=self.dup_sems[1].at[slot],
            device_id={"blk": ring.partner},
            device_id_type=MESH,
        )

    def start(self):
        for sign in (1, -1):
            self.copy(1, sign, False).start()
        if self.dup_sems is not None:
            self.dup(0, 1).start()

    def serve(self, distance):
        for sign in (1, -1):
            if distance <= self.hops[sign]:
                self.copy(distance, sign, True).wait_recv()
                if distance < self.hops[sign]:
                    self.copy(distance + 1, sign, False).start()
                if self.dup_sems is not None:
                    self.dup(distance, sign).start()

    def settle(self, distance):
        for sign in (1, -1) if distance else (1,):
            if distance <= self.hops[sign]:
                self.dup(distance, sign, True).wait_recv()

    def drain(self):
        for sign in (1, -1):
            for distance in range(1, self.hops[sign] + 1):
                self.copy(distance, sign, False).wait_send()
                if self.dup_sems is not None:
                    self.dup(distance, sign).wait_send()
        if self.dup_sems is not None:
            self.dup(0, 1).wait_send()


def turn(values, cosine, sine, lane):
    swapped = jnp.where(lane % HEAD < HEAD // 2, pltpu.roll(values, 2 * HEAD - HEAD // 2, 1), pltpu.roll(values, HEAD // 2, 1))
    return values * cosine + swapped * sine


def layer_kernel(n, hidden_ref, idx_ref, count_ref, norm_ref, router_ref, wq_ref, wk_ref, wv_ref,
                 wo_ref, gain_ref, rate_ref, final_ref,
                 normed_buf, meta_buf, metas_buf, x_buf, kvw_own, kvw_buf, wq_buf, wo_buf, q_acc, q_buf,
                 kv_own, kv_buf, pairs_buf, mask_buf, att_buf, out_buf, update_buf, cos_buf, sin_buf,
                 rows_send, rows_recv, meta_send, meta_recv, att_send, att_recv, out_send, out_recv,
                 w_send, w_recv, dup_send, dup_recv, a_send, a_recv):
    ring = Ring(n)
    chips, chip, core, group, me = ring.chips, ring.chip, ring.core, ring.group, ring.me
    other = 1 - group
    barrier = pltpu.get_barrier_semaphore()
    for device in ({"blk": ring.ahead}, {"blk": ring.behind}, {"blk": ring.partner},
                   {"groups": other}, {"groups": other, "blk": ring.partner}):
        pl.semaphore_signal(barrier, inc=1, device_id=device, device_id_type=MESH)
    tokens, width = hidden_ref.shape
    cap = idx_ref.shape[1]
    lanes = 2 * HEAD
    half = width // 2
    part = half // 2
    slots = 2 * cap
    keep = pairs_buf.shape[0]
    home_here = core == group

    def side(ref):
        return jnp.where(group == 0, ref[:, :HEAD].astype(jnp.float32), ref[:, HEAD:].astype(jnp.float32))

    kvw_own[...] = jnp.concatenate([side(wk_ref), side(wv_ref)], axis=1).astype(jnp.bfloat16)
    line = lax.broadcasted_iota(jnp.int32, meta_buf.shape, 0)
    meta_buf[...] = jnp.where(line == 0, idx_ref[...], count_ref[...])

    def columns(ref, k):
        return ref.at[:, pl.ds(pl.multiple_of(group * half + k * part, part), part)]

    rows_each = wq_ref.shape[0]
    kvw = Spread(ring, kvw_own, kvw_buf, rows_each, (w_send.at[0], w_recv.at[0]), (dup_send.at[0], dup_recv.at[0]))
    wq = [Spread(ring, columns(wq_ref, k), wq_buf.at[k], rows_each, (w_send.at[1 + k], w_recv.at[1 + k]),
                 (dup_send.at[1 + k], dup_recv.at[1 + k]), flip=k == 1) for k in range(2)]
    wo = [Spread(ring, columns(wo_ref, k), wo_buf.at[k], rows_each, (w_send.at[3 + k], w_recv.at[3 + k]),
                 (dup_send.at[3 + k], dup_recv.at[3 + k]), flip=k == 1) for k in range(2)]
    kv = Spread(ring, kv_own, kv_buf, slots, (a_send.at[0], a_recv.at[0]))
    own_metas = metas_buf.at[pl.ds(pl.multiple_of(chip * 2, 2), 2)]
    metas = Spread(ring, own_metas, metas_buf, 2, (a_send.at[1], a_recv.at[1]), flip=True)

    def to_seq(k):
        target = chip * 2 + group
        return {"blk": target} if k == 0 else {"groups": other, "blk": target}

    def rows_copy(k, j):
        return pltpu.make_async_remote_copy(
            src_ref=normed_buf, dst_ref=x_buf.at[j], send_sem=rows_send.at[k], recv_sem=rows_recv.at[j],
            device_id=to_seq(k), device_id_type=MESH)

    def meta_copy(k, j):
        return pltpu.make_async_remote_copy(
            src_ref=meta_buf, dst_ref=metas_buf.at[chip * 2 + j], send_sem=meta_send.at[k], recv_sem=meta_recv.at[j],
            device_id=to_seq(k), device_id_type=MESH)

    pl.semaphore_wait(barrier, 5)
    kvw.start()
    wq[0].start()
    wq[1].start()
    meta_copy(1, core).start()

    @pl.when(home_here)
    def _():
        metas_buf[chip * 2 + core] = meta_buf[...]

    @pl.when(jnp.logical_not(home_here))
    def _():
        meta_copy(0, core).start()

    pick = lax.broadcasted_iota(jnp.int32, (tokens, cap), 0) == idx_ref[...]
    token_rows = lax.dot_general(
        pick.astype(jnp.float32).astype(jnp.bfloat16),
        hidden_ref[...],
        (((0,), (0,)), ((), ())),
        preferred_element_type=jnp.float32,
    )
    final_ref[...] = token_rows.astype(jnp.bfloat16)
    normed_buf[...] = rms_scale(token_rows, norm_ref[...]).astype(jnp.bfloat16)
    rows_copy(1, core).start()

    @pl.when(home_here)
    def _():
        x_buf[core] = normed_buf[...]

    @pl.when(jnp.logical_not(home_here))
    def _():
        rows_copy(0, core).start()

    def arrived(copy):
        for j in range(2):
            @pl.when(jnp.logical_not(jnp.logical_and(home_here, core == j)))
            def _():
                copy(1, j).wait_recv()

    kvw.serve(1)
    arrived(meta_copy)
    metas.start()
    wq[0].serve(1)
    wq[1].serve(1)
    kvw.serve(2)
    metas.serve(1)
    kvw.serve(3)
    metas.serve(2)
    kvw.serve(4)
    metas.serve(3)
    wq[0].serve(2)
    wq[1].serve(2)
    metas.serve(4)
    for d in range(chips // 2 + 1):
        kvw.settle(d)

    lane = lax.broadcasted_iota(jnp.int32, (1, lanes), 1)
    sign = jnp.where(lane % HEAD < HEAD // 2, -1.0, 1.0)
    square_row = lax.broadcasted_iota(jnp.int32, (cap, cap), 0)
    square_col = lax.broadcasted_iota(jnp.int32, (cap, cap), 1)
    slot = lax.broadcasted_iota(jnp.int32, (1, cap), 1)
    for j in range(2):
        spots = (metas_buf[chip * 2 + j, 0:1, :] + (chip * 2 + j) * tokens).astype(jnp.float32)
        spot = jnp.sum(jnp.where(square_row == square_col, spots, 0.0), axis=1, keepdims=True)
        angle = spot * rate_ref[...]
        cos_buf[j * cap : (j + 1) * cap, :] = jnp.cos(angle)
        sin_buf[j * cap : (j + 1) * cap, :] = jnp.sin(angle) * sign
    starts, counts = [], []
    start = jnp.zeros((1, cap), jnp.int32)
    own_start = [jnp.zeros((1, cap), jnp.int32) for _ in range(2)]
    for s in range(n):
        count = metas_buf[s, 1:2, :]
        starts.append(start)
        counts.append(count)
        start = start + count
        for j in range(2):
            own_start[j] = own_start[j] + jnp.where(chip * 2 + j > s, count, 0)
    for j in range(2):
        for k in range(keep // cap):
            seen = square_col + k * cap - square_row <= own_start[j]
            mask_buf[j * cap : (j + 1) * cap, k * cap : (k + 1) * cap] = jnp.where(seen, 0.0, -1e30)

    arrived(rows_copy)
    kvw_buf[pl.ds(pl.multiple_of(me * rows_each, rows_each), rows_each)] = kvw_own[...]
    x_all = x_buf[...].reshape(slots, width)
    both = jnp.dot(x_all, kvw_buf[...], preferred_element_type=jnp.float32)
    gain = jnp.concatenate([gain_ref[1:2, :], gain_ref[1:2, :]], axis=1)
    mean = jnp.sum(jnp.where(lane < HEAD, both * both, 0.0), axis=1, keepdims=True) * (1.0 / HEAD)
    key = turn(both * lax.rsqrt(mean + norm_eps) * gain, cos_buf[...], sin_buf[...], lane)
    kv_own[...] = jnp.where(lane < HEAD, key, both).astype(jnp.bfloat16)
    kv.start()
    kv_buf[pl.ds(pl.multiple_of(chip * slots, slots), slots)] = kv_own[...]

    def own_rows(ref, buf, k):
        buf[k, pl.ds(pl.multiple_of(me * rows_each, rows_each), rows_each)] = columns(ref, k)[...]

    def q_block(distance, sgn):
        at = ring.chip_at(ring.place - sgn * distance) * (2 * rows_each)
        at = pl.ds(pl.multiple_of(at, 2 * rows_each), 2 * rows_each)
        source = x_buf[:, :, at].reshape(slots, 2 * rows_each)
        for k in range(2):
            cols = slice(k * part, (k + 1) * part)
            product = jnp.dot(source, wq_buf[k, at, :], preferred_element_type=jnp.float32)
            q_acc[:, cols] = product if distance == 0 else q_acc[:, cols] + product

    def q_wave(distance):
        for k in range(2):
            wq[k].settle(distance)
        for sgn in (1, -1) if 0 < distance < chips // 2 else (1,):
            q_block(distance, sgn)

    for k in range(2):
        own_rows(wq_ref, wq_buf, k)
        own_rows(wo_ref, wo_buf, k)
    q_wave(0)
    q_wave(1)
    wq[0].serve(3)
    wq[1].serve(3)
    wo[0].start()
    wo[1].start()
    kv.serve(1)
    q_wave(2)
    wq[0].serve(4)
    wq[1].serve(4)
    q_wave(3)
    kv.serve(2)
    q_wave(4)

    gain = jnp.concatenate([gain_ref[0:1, :], gain_ref[0:1, :]], axis=1) * (1.0 / math.sqrt(HEAD))

    def q_finish(p):
        total = q_acc[:, p * lanes : (p + 1) * lanes]
        squares = total * total
        first = jnp.sum(jnp.where(lane < HEAD, squares, 0.0), axis=1, keepdims=True)
        second = jnp.sum(jnp.where(lane < HEAD, 0.0, squares), axis=1, keepdims=True)
        mean = jnp.where(lane < HEAD, first, second) * (1.0 / HEAD)
        values = total * lax.rsqrt(mean + norm_eps) * gain
        values = turn(values, cos_buf[...], sin_buf[...], lane)
        q_buf[2 * p] = jnp.where(lane < HEAD, values, 0.0).astype(jnp.bfloat16)
        q_buf[2 * p + 1] = jnp.where(lane < HEAD, pltpu.roll(values, HEAD, 1), 0.0).astype(jnp.bfloat16)

    heads = half // HEAD
    for p in range(heads // 2):
        q_finish(p)
    wo[0].serve(1)
    wo[1].serve(1)
    kv.serve(3)
    kv.serve(4)
    blocks = keep // cap
    for k in range(blocks):
        begin, end = k, min(n, k + n - blocks + 1)
        hits = []
        for s in range(begin, end):
            ranks = jnp.where(slot < counts[s], starts[s] + slot, -1)
            hits.append((square_row + k * cap == ranks).astype(jnp.float32).astype(jnp.bfloat16))
        dense = jnp.dot(jnp.concatenate(hits, axis=1), kv_buf[begin * cap : end * cap, :], preferred_element_type=jnp.float32)
        pairs_buf[k * cap : (k + 1) * cap, :] = dense.astype(jnp.bfloat16)

    def attend_head(h):
        scores = lax.dot_general(
            q_buf[h], pairs_buf[...], (((1,), (1,)), ((), ())), preferred_element_type=jnp.float32
        ) + mask_buf[...]
        top = jnp.max(scores, axis=-1, keepdims=True)
        weights = jnp.exp(scores - top)
        denominator = jnp.sum(weights, axis=-1, keepdims=True)
        mix = jnp.dot(weights.astype(jnp.bfloat16), pairs_buf[...], preferred_element_type=jnp.float32)
        return mix / denominator

    def att_copy(i, source):
        at = att_buf.at[source * (chips // 2) + i]
        return pltpu.make_async_remote_copy(
            src_ref=at, dst_ref=at, send_sem=att_send.at[i], recv_sem=att_recv.at[i],
            device_id={"groups": other}, device_id_type=MESH)

    chunk_heads = heads // (chips // 2)
    for i in range(chips // 2):
        for p in range(chunk_heads // 2):
            mixes = [attend_head(i * chunk_heads + 2 * p + e) for e in range(2)]
            joined = jnp.where(lane < HEAD, pltpu.roll(mixes[0], HEAD, 1), mixes[1])
            att_buf[group * (chips // 2) + i, :, p * lanes : (p + 1) * lanes] = joined.astype(jnp.bfloat16)
        att_copy(i, group).start()
        if i + 2 <= chips // 2:
            wo[0].serve(i + 2)
            wo[1].serve(i + 2)

    for i in range(chips // 2):
        att_copy(i, other).wait_recv()
    for k in range(2):
        for d in range(chips // 2 + 1):
            wo[k].settle(d)

    def out_copy(k, j, here):
        target = chip * 2 + j
        return pltpu.make_async_remote_copy(
            src_ref=out_buf.at[k, j], dst_ref=update_buf.at[group, k], send_sem=out_send.at[k, j], recv_sem=out_recv.at[group, k],
            device_id={"blk": target} if here else {"groups": other, "blk": target}, device_id_type=MESH)

    for k in range(2):
        total = None
        for i in range(chips):
            product = jnp.dot(att_buf[i], wo_buf[k, i * 2 * rows_each : (i + 1) * 2 * rows_each, :], preferred_element_type=jnp.float32)
            total = product if total is None else total + product
        out_buf[k] = total.astype(jnp.bfloat16).reshape(2, cap, part)

        @pl.when(home_here)
        def _():
            update_buf[group, k] = out_buf[k, core]
            out_copy(k, 1 - core, True).start()

        @pl.when(jnp.logical_not(home_here))
        def _():
            for j in range(2):
                out_copy(k, j, False).start()

    rows = final_ref[...].astype(jnp.float32)
    gate = jax.nn.sigmoid(jnp.sum(rows * router_ref[...].astype(jnp.float32), axis=1, keepdims=True))

    def update_wait(h, k):
        pltpu.make_async_remote_copy(
            src_ref=out_buf.at[k, 0], dst_ref=update_buf.at[h, k], send_sem=out_send.at[k, 0], recv_sem=out_recv.at[h, k],
            device_id={"groups": other}, device_id_type=MESH).wait_recv()

    for k in range(2):
        update_wait(other, k)

        @pl.when(jnp.logical_not(home_here))
        def _():
            update_wait(group, k)

        for h in range(2):
            cols = slice(h * half + k * part, h * half + (k + 1) * part)
            final_ref[:, cols] = (rows[:, cols] + gate * update_buf[h, k].astype(jnp.float32)).astype(jnp.bfloat16)

    for item in [kvw, kv, metas] + wq + wo:
        item.drain()
    for i in range(chips // 2):
        att_copy(i, group).wait_send()
    rows_copy(1, core).wait_send()
    meta_copy(1, core).wait_send()

    @pl.when(home_here)
    def _():
        for k in range(2):
            out_copy(k, 1 - core, True).wait_send()

    @pl.when(jnp.logical_not(home_here))
    def _():
        rows_copy(0, core).wait_send()
        meta_copy(0, core).wait_send()
        for k in range(2):
            for j in range(2):
                out_copy(k, j, False).wait_send()


def layer(n, keep, hidden, kept_idx, kept_count, router, norm_gain, qk_gain, query_weight, key_weight,
          value_weight, out_weight):
    tokens, width = hidden.shape
    cap = kept_idx.shape[1]
    lanes, chips = 2 * HEAD, n // 2
    half, part, slots = width // 2, width // 4, 2 * cap
    rows_each = query_weight.shape[0]
    half_size = HEAD // 2
    rates = rope_base ** (-(np.arange(half_size) * 2.0 / HEAD))
    rates = np.tile(rates, lanes // half_size)[None, :].astype(np.float32)
    dma = pltpu.SemaphoreType.DMA
    return pl.pallas_call(
        functools.partial(layer_kernel, n),
        out_shape=jax.ShapeDtypeStruct((cap, width), jnp.bfloat16),
        in_specs=[VM] * 11,
        out_specs=VM,
        scratch_shapes=[
            pltpu.VMEM((cap, width), jnp.bfloat16),
            pltpu.VMEM((8, cap), jnp.int32),
            pltpu.VMEM((n, 8, cap), jnp.int32),
            pltpu.VMEM((2, cap, width), jnp.bfloat16),
            pltpu.VMEM((rows_each, lanes), jnp.bfloat16),
            pltpu.VMEM((width, lanes), jnp.bfloat16),
            pltpu.VMEM((2, width, part), jnp.bfloat16),
            pltpu.VMEM((2, width, part), jnp.bfloat16),
            pltpu.VMEM((slots, half), jnp.float32),
            pltpu.VMEM((half // HEAD, slots, lanes), jnp.bfloat16),
            pltpu.VMEM((slots, lanes), jnp.bfloat16),
            pltpu.VMEM((n * cap, lanes), jnp.bfloat16),
            pltpu.VMEM((keep, lanes), jnp.bfloat16),
            pltpu.VMEM((slots, keep), jnp.float32),
            pltpu.VMEM((chips, slots, width // chips), jnp.bfloat16),
            pltpu.VMEM((2, 2, cap, part), jnp.bfloat16),
            pltpu.VMEM((2, 2, cap, part), jnp.bfloat16),
            pltpu.VMEM((slots, lanes), jnp.float32),
            pltpu.VMEM((slots, lanes), jnp.float32),
            dma((2,)), dma((2,)), dma((2,)), dma((2,)),
            dma((chips // 2,)), dma((chips // 2,)), dma((2, 2)), dma((2, 2)),
        ]
        + Spread.semaphores(chips, 5)
        + [dma((5, chips)), dma((5, chips))]
        + Spread.semaphores(chips, 2),
        compiler_params=pltpu.CompilerParams(collective_id=1, has_side_effects=True),
    )(
        hidden, kept_idx, kept_count.reshape(1, 1), norm_gain.reshape(1, width), router.reshape(1, width),
        query_weight, key_weight, value_weight, out_weight, qk_gain, rates,
    )


def body(
    n,
    hidden,
    kept_idx,
    kept_count,
    router,
    norm_gain,
    qk_gain,
    query_weight,
    key_weight,
    value_weight,
    out_weight,
):
    tokens = hidden.shape[0]
    cap = kept_idx.shape[1]
    keep = n * (tokens * KEEP_DEV // TOK_DEV)
    final = layer(
        n, keep, hidden, kept_idx, kept_count, router, norm_gain, qk_gain, query_weight, key_weight,
        value_weight, out_weight,
    )
    slots = jnp.arange(cap, dtype=jnp.int32)
    put = (kept_idx == jnp.arange(tokens, dtype=jnp.int32)[:, None]) & (slots[None, :] < kept_count[0])
    placed = jnp.dot(put.astype(jnp.bfloat16), final, preferred_element_type=jnp.float32)
    return jnp.where(jnp.any(put, axis=1)[:, None], placed.astype(jnp.bfloat16), hidden)


def attend(query_heads, query_ranks, key_block, value_block, key_ranks, state):
    prev_top, prev_total, prev_acc = state
    length = key_block.shape[0]
    keys_split = key_block.reshape(length, KV_HEADS, HEAD)
    values_split = value_block.reshape(length, KV_HEADS, HEAD)
    scores = jnp.einsum(
        "agch,bgh->gcab", query_heads, keys_split, preferred_element_type=jnp.float32
    ) * (1.0 / math.sqrt(HEAD))
    allowed = key_ranks[None, :] <= query_ranks[:, None]
    masked = jnp.where(allowed, scores, -1e30)
    new_top = jnp.maximum(prev_top, jnp.max(masked, axis=-1))
    weights = jnp.where(allowed, jnp.exp(masked - new_top[..., None]), 0.0)
    factor = jnp.exp(prev_top - new_top)
    new_total = prev_total * factor + jnp.sum(weights, axis=-1)
    new_acc = prev_acc * factor[..., None] + jnp.einsum(
        "gcab,bgh->gcah",
        weights.astype(jnp.bfloat16),
        values_split,
        preferred_element_type=jnp.float32,
    )
    return (new_top, new_total, new_acc)


def make_fold(query_heads, query_ranks, rank_of, state, pieces):
    key_piece, value_piece = pieces
    length = key_piece.shape[0]

    def inner(block_turn, inner_state):
        block_start = block_turn * 512
        key_block = lax.dynamic_slice_in_dim(key_piece, block_start, 512, 0)
        value_block = lax.dynamic_slice_in_dim(value_piece, block_start, 512, 0)
        key_ranks = rank_of(block_start + jnp.arange(512, dtype=jnp.int32))
        return attend(query_heads, query_ranks, key_block, value_block, key_ranks, inner_state)

    return lax.fori_loop(0, length // 512, inner, state)


def wide_body(
    hidden,
    kept_idx,
    kept_count,
    router,
    norm_gain,
    qk_gain,
    query_weight,
    key_weight,
    value_weight,
    out_weight,
):
    shard_count = lax.axis_size("blk")
    device = lax.axis_index("blk")
    width = hidden.shape[1]
    all_lists, all_counts = (
        lax.all_gather(kept_idx, "blk", axis=0, tiled=True),
        lax.all_gather(kept_count, "blk", axis=0, tiled=True),
    )
    starts = jnp.cumsum(all_counts) - all_counts
    own_start = starts[device]
    own_count = all_counts[device]
    list_slots = jnp.arange(CAP, dtype=jnp.int32)
    is_valid = list_slots < own_count
    token_rows = hidden[kept_idx[0]]
    gate_value = jax.nn.sigmoid(jnp.dot(token_rows, router, preferred_element_type=jnp.float32))
    slot_count = (CAP + shard_count - 1) // shard_count
    outgoing = jnp.where(is_valid[:, None], token_rows, jnp.zeros_like(token_rows))
    outgoing = jnp.roll(outgoing.reshape(slot_count, shard_count, width), own_start, axis=1)
    incoming = lax.all_to_all(outgoing, "blk", split_axis=1, concat_axis=1, tiled=True)
    query_ranks = device + jnp.arange(KEEP_DEV, dtype=jnp.int32) * shard_count
    source_ends = starts + all_counts
    source = jnp.sum((source_ends[None, :] <= query_ranks[:, None]).astype(jnp.int32), axis=1)
    within = query_ranks - starts[source]
    flat_index = within // shard_count * shard_count + source
    kept_rows = incoming.reshape(slot_count * shard_count, width)[flat_index]
    positions = source * TOK_DEV + all_lists[source, within]
    row_total = kept_rows.shape[0]
    normed = rms_scale(kept_rows.astype(jnp.float32), norm_gain).astype(jnp.bfloat16)
    query_cols = Q_HEADS * HEAD
    kv_cols = KV_HEADS * HEAD
    full_query, full_key, full_value, full_out = (
        lax.all_gather(query_weight, "blk", axis=0, tiled=True),
        lax.all_gather(key_weight, "blk", axis=0, tiled=True),
        lax.all_gather(value_weight, "blk", axis=0, tiled=True),
        lax.all_gather(out_weight, "blk", axis=0, tiled=True),
    )
    query_lin = jnp.dot(normed, full_query, preferred_element_type=jnp.float32)
    key_lin = jnp.dot(normed, full_key, preferred_element_type=jnp.float32)
    value_lin = jnp.dot(normed, full_value, preferred_element_type=jnp.float32)
    half_size = HEAD // 2
    rotation_rates = rope_base ** (-(jnp.arange(half_size, dtype=jnp.float32) * 2.0 / HEAD))
    angles = (positions.astype(jnp.float32)[:, None] * rotation_rates[None, :])[:, None, :]
    query_heads = rotate(
        rms_scale(query_lin.reshape(row_total, Q_HEADS, HEAD), qk_gain[0]), angles
    ).astype(jnp.bfloat16)
    key_heads = rotate(
        rms_scale(key_lin.reshape(row_total, KV_HEADS, HEAD), qk_gain[1]), angles
    ).astype(jnp.bfloat16)
    query_heads = query_heads.reshape(row_total, KV_HEADS, Q_HEADS // KV_HEADS, HEAD)
    key_flat = key_heads.reshape(row_total, kv_cols)
    value_flat = value_lin.astype(jnp.bfloat16)
    group_size = Q_HEADS // KV_HEADS
    start_state = (
        jnp.full((KV_HEADS, group_size, row_total), -1e30, jnp.float32),
        jnp.zeros((KV_HEADS, group_size, row_total), jnp.float32),
        jnp.zeros((KV_HEADS, group_size, row_total, HEAD), jnp.float32),
    )

    def strided_rank(slots_seen):
        return slots_seen // KEEP_DEV + slots_seen % KEEP_DEV * shard_count

    final_top, final_total, final_acc = make_fold(
        query_heads,
        query_ranks,
        strided_rank,
        start_state,
        (
            lax.all_gather(key_flat, "blk", axis=0, tiled=True),
            lax.all_gather(value_flat, "blk", axis=0, tiled=True),
        ),
    )
    attended = (
        (final_acc / final_total[..., None])
        .transpose(2, 0, 1, 3)
        .reshape(row_total, query_cols)
        .astype(jnp.bfloat16)
    )
    update = jnp.dot(attended, full_out, preferred_element_type=jnp.float32)
    update = update.astype(jnp.bfloat16)
    slot_grid = (
        jnp.arange(slot_count, dtype=jnp.int32)[:, None] * shard_count
        + jnp.mod(device - starts, shard_count)[None, :]
    )
    back_valid = slot_grid < all_counts[None, :]
    local_place = (starts[None, :] + slot_grid - device) // shard_count
    clipped = jnp.where(back_valid, local_place, 0)
    back_rows = jnp.where(back_valid[..., None], update[clipped], jnp.zeros((), jnp.bfloat16))
    returned = lax.all_to_all(back_rows, "blk", split_axis=1, concat_axis=1, tiled=True)
    returned = jnp.roll(returned, -own_start, axis=1).reshape(slot_count * shard_count, width)
    final = (
        token_rows.astype(jnp.float32) + gate_value[:, None] * returned.astype(jnp.float32)
    ).astype(jnp.bfloat16)
    target = jnp.where(is_valid, kept_idx[0], TOK_DEV)
    return hidden.at[target].set(final, mode="drop")


def solution(mesh):
    placed = (
        P(("groups", "blk"), None),
        P(("groups", "blk"), None),
        P(("groups", "blk")),
        P(),
        P(),
        P(),
        P("blk", None),
        P("blk", None),
        P("blk", None),
        P("blk", None),
    )
    n = mesh.shape["blk"]
    by_heads = n % 4 == 0 and Q_HEADS == 2 * n and mesh.shape["groups"] == KV_HEADS
    step = functools.partial(body, n) if by_heads else wide_body
    return jax.shard_map(
        step, mesh=mesh, in_specs=placed, out_specs=P(("groups", "blk"), None), check_vma=False
    )
```

```python
import functools
import math

import jax
import jax.numpy as jnp
import numpy as np
from jax import lax
from jax.experimental import pallas as pl
from jax.experimental.pallas import tpu as pltpu
from jax.sharding import PartitionSpec as P

Q_HEADS = 32
KV_HEADS = 2
HEAD = 64
TOK_DEV = 512
KEEP_DEV = 64
CAP = 128
MESH = pl.DeviceIdType.MESH
ANY = pl.BlockSpec(memory_space=pl.ANY)
HBM = pl.BlockSpec(memory_space=pltpu.HBM)


norm_eps = 1e-06
rope_base = 1000000.0


def rms_scale(values, scales):
    return values * lax.rsqrt(jnp.mean(values * values, axis=-1, keepdims=True) + norm_eps) * scales


def rotate(values, angles):
    half_size = values.shape[-1] // 2
    lower_half = values[..., :half_size]
    upper_half = values[..., half_size:]
    cosine = jnp.cos(angles)
    sine_part = jnp.sin(angles)
    return jnp.concatenate(
        [
            lower_half * cosine - upper_half * sine_part,
            upper_half * cosine + lower_half * sine_part,
        ],
        axis=-1,
    )


class Place:
    def __init__(self, n):
        self.depth = n // 4
        self.me = lax.axis_index("blk")
        self.group = lax.axis_index("groups")
        self.chip, self.core = self.me // 2, self.me % 2
        self.z, self.y = self.chip // 2, self.chip % 2
        self.partner = self.chip * 2 + 1 - self.core
        self.across = (self.chip + 1 - 2 * self.y) * 2

    def inside(self, z):
        return jnp.logical_and(z >= 0, z < self.depth)


def remote(source, target, send, recv, device):
    return pltpu.make_async_remote_copy(
        src_ref=source, dst_ref=target, send_sem=send, recv_sem=recv, device_id=device, device_id_type=MESH
    )


class Line:
    direct = True

    def __init__(self, place, own, buf, rows, view, sems):
        self.place, self.own, self.buf, self.rows, self.view = place, own, buf, rows, view
        self.z_send, self.z_recv, self.dup_send, self.dup_recv = sems
        self.dups = place.depth

    @staticmethod
    def semaphores(depth, count):
        dma = pltpu.SemaphoreType.DMA
        return [dma((count,)), dma((count, depth)), dma((count,)), dma((count,))]

    def along(self, source, z, offset):
        p = self.place
        return remote(source, self.view(z, p.core), self.z_send, self.z_recv.at[z], {"blk": p.me + 4 * offset})

    def dup(self, source, target):
        return remote(source, target, self.dup_send, self.dup_recv, {"blk": self.place.partner})

    def launch(self, source):
        p = self.place
        for offset in range(1, p.depth if self.direct else 2):
            for sign in (1, -1):
                @pl.when(p.inside(p.z + sign * offset))
                def _():
                    self.along(source, p.z, sign * offset).start()

    def start(self):
        p = self.place
        self.launch(self.own)
        self.dup(self.own, self.view(p.z, p.core)).start()

    def passed(self, z):
        pass

    def serve(self, distance):
        p = self.place
        for sign in (1, -1):
            z = p.z - sign * distance

            @pl.when(p.inside(z))
            def _():
                block = self.view(z, p.core)
                self.along(block, z, sign).wait_recv()
                if not self.direct:
                    @pl.when(p.inside(p.z + sign))
                    def _():
                        self.along(block, z, sign).start()

                self.passed(z)
                self.dup(block, block).start()

    def serve_all(self):
        for distance in range(1, self.place.depth):
            self.serve(distance)

    def total(self, blocks):
        return self.buf.at[pl.ds(0, blocks * self.rows)]

    def settle(self):
        whole = self.total(self.dups)
        self.dup(whole, whole).wait_recv()

    def drain(self):
        p = self.place

        def sent(blocks):
            whole = self.total(blocks)
            remote(whole, whole, self.z_send, self.z_recv.at[0], {"blk": p.partner}).wait_send()

        if self.direct:
            sent(p.depth - 1)
        else:
            middle = jnp.logical_and(p.z > 0, p.z < p.depth - 1)
            pl.when(middle)(lambda: sent(p.depth + 1))
            pl.when(jnp.logical_not(middle))(lambda: sent(1))
        whole = self.total(self.dups)
        self.dup(whole, whole).wait_send()


class Weight(Line):
    def __init__(self, place, mine, theirs, buf, sems, direct=False):
        self.place, self.mine, self.theirs, self.buf, self.direct = place, mine, theirs, buf, direct
        self.rows = mine.shape[0]
        self.z_send, self.z_recv, self.dup_send, self.dup_recv = sems[:4]
        self.side_recv, self.side_send, self.x_recv = sems[4:]
        self.dups = 2 * place.depth

    @staticmethod
    def semaphores(depth, count):
        dma = pltpu.SemaphoreType.DMA
        return Line.semaphores(depth, count) + [dma((count,)), dma((count,)), dma((count, depth))]

    def block(self, z, y, core):
        at = (4 * z + 2 * y + core) * self.rows
        return self.buf.at[pl.ds(pl.multiple_of(at, self.rows), self.rows)]

    def view(self, z, core):
        return self.block(z, self.place.group, core)

    def side(self, y):
        p = self.place
        return remote(self.theirs, self.block(p.z, y, p.core), self.side_send, self.side_recv, {"blk": p.across + p.core})

    def other(self, z, group):
        block = self.block(z, group, self.place.core)
        return remote(block, block, self.side_send, self.x_recv.at[z], {"groups": 1 - self.place.group})

    def start_side(self):
        self.side(self.place.y).start()

    def start(self):
        p = self.place

        @pl.when(p.y == p.group)
        def _():
            self.launch(self.mine)

        self.dup(self.mine, self.block(p.z, p.y, p.core)).start()

    def keep(self, sem):
        p = self.place
        return pltpu.make_async_copy(self.mine, self.block(p.z, p.y, p.core), sem)

    def sided(self):
        p = self.place
        block = self.block(p.z, 1 - p.y, p.core)
        self.side(1 - p.y).wait_recv()

        @pl.when(p.y != p.group)
        def _():
            self.launch(block)

        self.dup(block, block).start()

    def passed(self, z):
        self.other(z, self.place.group).start()

    def cross(self, distance):
        p = self.place
        for sign in (1, -1):
            z = p.z - sign * distance

            @pl.when(p.inside(z))
            def _():
                self.other(z, 1 - p.group).wait_recv()
                block = self.block(z, 1 - p.group, p.core)
                self.dup(block, block).start()

    def cross_all(self):
        for distance in range(1, self.place.depth):
            self.cross(distance)

    def drain(self):
        super().drain()
        whole = self.total(self.place.depth)
        remote(whole, whole, self.side_send, self.side_recv, {"blk": self.place.partner}).wait_send()


def turn(values, cosine, sine, lane):
    swapped = jnp.where(lane % HEAD < HEAD // 2, pltpu.roll(values, 2 * HEAD - HEAD // 2, 1), pltpu.roll(values, HEAD // 2, 1))
    return values * cosine + swapped * sine


def layer_kernel(n, pieces, hidden_ref, wq_ref, wo_ref, idx_hbm, count_hbm, norm_hbm, router_hbm, wk_hbm, wv_hbm,
                 gain_hbm, rate_hbm, out_ref, idx_ref, count_ref, norm_ref, router_ref, wk_ref, wv_ref, gain_ref, rate_ref,
                 small_sem, final_ref, placed_buf, placed_sem,
                 normed_buf, meta_buf, metas_buf, x_buf, kvw_own, kvw_buf, wq_buf, wo_buf, q_buf,
                 kv_own, kv_buf, pairs_buf, mask_buf, att_buf, out_buf, update_buf, cos_buf, sin_buf,
                 rows_send, rows_recv, meta_send, meta_recv, att_send, att_recv, out_send, out_recv, keep_sem, load_sem, hidden_buf, *sems):
    p = Place(n)
    depth, chip, core, y, me = p.depth, p.chip, p.core, p.y, p.me
    chips = n // 2
    barrier = pltpu.get_barrier_semaphore()
    for device in ({"blk": p.partner}, {"blk": p.across}, {"blk": p.across + 1}, {"groups": 1 - p.group}):
        pl.semaphore_signal(barrier, inc=1, device_id=device, device_id_type=MESH)
    for offset in range(1, depth):
        for sign in (1, -1):
            @pl.when(p.inside(p.z + sign * offset))
            def _():
                pl.semaphore_signal(barrier, inc=1, device_id={"blk": me + 4 * sign * offset}, device_id_type=MESH)
    load = pltpu.make_async_copy(hidden_ref, hidden_buf, load_sem)
    load.start()
    small = [pltpu.make_async_copy(source, target, small_sem.at[k]) for k, (source, target) in enumerate((
        (idx_hbm, idx_ref), (count_hbm, count_ref), (wk_hbm, wk_ref), (wv_hbm, wv_ref), (norm_hbm, norm_ref),
        (gain_hbm, gain_ref), (rate_hbm, rate_ref), (router_hbm, router_ref)))]
    for copy in small:
        copy.start()
    for item in small:
        item.wait()
    tokens, width = hidden_ref.shape
    cap = idx_ref.shape[1]
    lanes = 2 * HEAD
    half = width // 2
    part = half // pieces
    slots = 2 * cap
    keep = pairs_buf.shape[0]
    home_here = core == y
    away = jnp.logical_not(home_here)
    first_shard = 4 * p.z + 2 * core

    def head_side(ref, of):
        return jnp.where(of == 0, ref[:, :HEAD].astype(jnp.float32), ref[:, HEAD:].astype(jnp.float32))

    for k, of in enumerate((y, 1 - y)):
        kvw_own[k] = jnp.concatenate([head_side(wk_ref, of), head_side(wv_ref, of)], axis=1).astype(jnp.bfloat16)
    line = lax.broadcasted_iota(jnp.int32, meta_buf.shape, 0)
    meta_buf[...] = jnp.where(line == 0, idx_ref[...], count_ref[...])

    def columns(ref, of, k):
        return ref.at[:, pl.ds(pl.multiple_of(of * half + k * part, part), part)]

    rows_each = wq_ref.shape[0]

    def take(sems, i):
        return [s.at[i] for s in sems]

    w_sems, a_sems = sems[:7], sems[7:]
    kvw = Weight(p, kvw_own.at[0], kvw_own.at[1], kvw_buf, take(w_sems, 0), direct=True)
    wq = [Weight(p, columns(wq_ref, y, k), columns(wq_ref, 1 - y, k), wq_buf.at[k], take(w_sems, 1 + k))
          for k in range(pieces)]
    wo = [Weight(p, columns(wo_ref, y, k), columns(wo_ref, 1 - y, k), wo_buf.at[k], take(w_sems, 1 + pieces + k))
          for k in range(pieces)]

    def pair_of(buf, each):
        def view(z, of):
            return buf.at[pl.ds(pl.multiple_of((4 * z + 2 * of) * each, 2 * each), 2 * each)]
        return view

    kv = Line(p, kv_own, kv_buf, slots, pair_of(kv_buf, cap), take(a_sems, 0))
    metas_view = pair_of(metas_buf, 1)
    metas = Line(p, metas_view(p.z, core), metas_buf, 2, metas_view, take(a_sems, 1))

    def worker(k):
        return {"blk": chip * 2 + y if k == 0 else p.across + y}

    def rows_copy(k, j):
        return remote(normed_buf, x_buf.at[j], rows_send.at[k], rows_recv.at[j], worker(k))

    def meta_copy(k, j):
        return remote(meta_buf, metas_buf.at[first_shard_of(k) + j], meta_send.at[k], meta_recv.at[j], worker(k))

    def first_shard_of(k):
        return 4 * p.z + 2 * y

    def meta_wait(k, j):
        return remote(meta_buf, metas_buf.at[first_shard + j], meta_send.at[k], meta_recv.at[j], worker(k))

    def arrived(copy):
        for j in range(2):
            @pl.when(jnp.logical_not(jnp.logical_and(home_here, core == j)))
            def _():
                copy(1, j).wait_recv()

    for item in wq + wo:
        item.keep(keep_sem).start()
    pl.semaphore_wait(barrier, 4 + depth - 1)
    first = wq + [kvw]
    for item in first:
        item.start_side()
    for item in first:
        item.start()
    meta_copy(1, core).start()

    @pl.when(home_here)
    def _():
        metas_buf[first_shard + core] = meta_buf[...]

    @pl.when(away)
    def _():
        meta_copy(0, core).start()

    load.wait()
    pick = lax.broadcasted_iota(jnp.int32, (tokens, cap), 0) == idx_ref[...]
    token_rows = lax.dot_general(
        pick.astype(jnp.float32).astype(jnp.bfloat16),
        hidden_buf[...],
        (((0,), (0,)), ((), ())),
        preferred_element_type=jnp.float32,
    )
    final_ref[...] = token_rows.astype(jnp.bfloat16)
    normed_buf[...] = rms_scale(token_rows, norm_ref[...]).astype(jnp.bfloat16)
    rows_copy(1, core).start()

    @pl.when(home_here)
    def _():
        x_buf[core] = normed_buf[...]

    @pl.when(away)
    def _():
        rows_copy(0, core).start()

    for item in wo:
        item.start_side()
    direct_line = y == p.group

    @pl.when(direct_line)
    def _():
        wq[0].serve(1)
        wq[1].serve(1)
        wq[0].sided()
        wq[2].serve(1)
        wq[1].sided()
        wq[3].serve(1)
        wq[2].sided()
        wq[3].sided()
        kvw.sided()
        kvw.serve_all()

    @pl.when(jnp.logical_not(direct_line))
    def _():
        wq[0].sided()
        wq[1].sided()
        wq[2].sided()
        wq[3].sided()
        kvw.sided()
        wq[0].serve(1)
        wq[1].serve(1)
        wq[2].serve(1)
        wq[3].serve(1)
        kvw.serve_all()

    arrived(meta_wait)
    wq[0].serve(2)
    wq[1].serve(2)
    metas.start()
    wq[2].serve(2)
    wq[3].serve(2)
    wo[0].start()
    wo[1].start()
    kvw.cross_all()
    metas.serve_all()

    lane = lax.broadcasted_iota(jnp.int32, (1, lanes), 1)
    sign_row = jnp.where(lane % HEAD < HEAD // 2, -1.0, 1.0)
    square_row = lax.broadcasted_iota(jnp.int32, (cap, cap), 0)
    square_col = lax.broadcasted_iota(jnp.int32, (cap, cap), 1)
    slot = lax.broadcasted_iota(jnp.int32, (1, cap), 1)
    wq[0].cross(1)
    wq[1].cross(1)
    wq[0].serve(3)
    wq[1].serve(3)
    for j in range(2):
        spots = (metas_buf[first_shard + j, 0:1, :] + (first_shard + j) * tokens).astype(jnp.float32)
        spot = jnp.sum(jnp.where(square_row == square_col, spots, 0.0), axis=1, keepdims=True)
        angle = spot * rate_ref[...]
        cos_buf[j * cap : (j + 1) * cap, :] = jnp.cos(angle)
        sin_buf[j * cap : (j + 1) * cap, :] = jnp.sin(angle) * sign_row
    wq[2].cross(1)
    wq[3].cross(1)
    arrived(rows_copy)
    kept = wq_buf.at[0, pl.ds(0, 2 * pieces * rows_each)]
    pltpu.make_async_copy(kept, kept, keep_sem).wait()
    kvw_buf[pl.ds(pl.multiple_of(me * rows_each, rows_each), rows_each)] = kvw_own[0]
    kvw.settle()
    x_all = x_buf[...].reshape(slots, width)
    both = jnp.dot(x_all, kvw_buf[...], preferred_element_type=jnp.float32)
    gain = jnp.concatenate([gain_ref[1:2, :], gain_ref[1:2, :]], axis=1)
    mean = jnp.sum(jnp.where(lane < HEAD, both * both, 0.0), axis=1, keepdims=True) * (1.0 / HEAD)
    key = turn(both * lax.rsqrt(mean + norm_eps) * gain, cos_buf[...], sin_buf[...], lane)
    kv_own[...] = jnp.where(lane < HEAD, key, both).astype(jnp.bfloat16)
    wq[2].serve(3)
    wq[3].serve(3)
    wo[0].sided()
    wo[1].sided()
    kv.start()
    kv_buf[pl.ds(pl.multiple_of(first_shard * cap, slots), slots)] = kv_own[...]

    q_gain = jnp.concatenate([gain_ref[0:1, :], gain_ref[0:1, :]], axis=1) * (1.0 / math.sqrt(HEAD))

    def q_piece(k):
        wq[k].settle()
        lin = jnp.dot(x_buf[...].reshape(slots, width), wq_buf[k], preferred_element_type=jnp.float32)
        for t in range(part // lanes):
            total = lin[:, t * lanes : (t + 1) * lanes]
            squares = total * total
            first = jnp.sum(jnp.where(lane < HEAD, squares, 0.0), axis=1, keepdims=True)
            second = jnp.sum(jnp.where(lane < HEAD, 0.0, squares), axis=1, keepdims=True)
            mean = jnp.where(lane < HEAD, first, second) * (1.0 / HEAD)
            values = total * lax.rsqrt(mean + norm_eps) * q_gain
            values = turn(values, cos_buf[...], sin_buf[...], lane)
            h = 2 * (k * (part // lanes) + t)
            q_buf[h] = jnp.where(lane < HEAD, values, 0.0).astype(jnp.bfloat16)
            q_buf[h + 1] = jnp.where(lane < HEAD, pltpu.roll(values, HEAD, 1), 0.0).astype(jnp.bfloat16)

    wq[0].cross(2)
    wq[1].cross(2)
    wo[2].start()
    wo[3].start()
    wo[2].sided()
    wq[2].cross(2)
    wq[3].cross(2)
    wo[3].sided()
    wq[0].cross(3)
    wq[1].cross(3)
    wo[0].serve(1)
    wq[2].cross(3)
    wq[3].cross(3)
    q_piece(0)
    wo[1].serve(1)
    q_piece(1)
    wo[2].serve(1)
    metas.settle()
    starts, counts = [], []
    start = jnp.zeros((1, cap), jnp.int32)
    own_start = [jnp.zeros((1, cap), jnp.int32) for _ in range(2)]
    for s in range(n):
        count = metas_buf[s, 1:2, :]
        starts.append(start)
        counts.append(count)
        start = start + count
        for j in range(2):
            own_start[j] = own_start[j] + jnp.where(first_shard + j > s, count, 0)
    for j in range(2):
        for k in range(keep // cap):
            seen = square_col + k * cap - square_row <= own_start[j]
            mask_buf[j * cap : (j + 1) * cap, k * cap : (k + 1) * cap] = jnp.where(seen, 0.0, -1e30)

    q_piece(2)
    wo[3].serve(1)
    q_piece(3)
    kv.serve_all()
    kv.settle()
    blocks = keep // cap
    for k in range(blocks):
        begin, end = k, min(n, k + n - blocks + 1)
        hits = []
        for s in range(begin, end):
            ranks = jnp.where(slot < counts[s], starts[s] + slot, -1)
            hits.append((square_row + k * cap == ranks).astype(jnp.float32).astype(jnp.bfloat16))
        dense = jnp.dot(jnp.concatenate(hits, axis=1), kv_buf[begin * cap : end * cap, :], preferred_element_type=jnp.float32)
        pairs_buf[k * cap : (k + 1) * cap, :] = dense.astype(jnp.bfloat16)

    def attend_head(h):
        scores = lax.dot_general(
            q_buf[h], pairs_buf[...], (((1,), (1,)), ((), ())), preferred_element_type=jnp.float32
        ) + mask_buf[...]
        top = jnp.max(scores, axis=-1, keepdims=True)
        weights = jnp.exp(scores - top)
        denominator = jnp.sum(weights, axis=-1, keepdims=True)
        mix = jnp.dot(weights.astype(jnp.bfloat16), pairs_buf[...], preferred_element_type=jnp.float32)
        return mix / denominator

    groups = chips // 2

    def att_copy(i, source):
        at = att_buf.at[source * groups + i]
        return remote(at, at, att_send, att_recv, {"blk": p.across + core})

    heads = half // HEAD
    chunk_heads = heads // groups

    def attend_pair(t):
        mixes = [attend_head(2 * t + e) for e in range(2)]
        joined = jnp.where(lane < HEAD, pltpu.roll(mixes[0], HEAD, 1), mixes[1])
        per = chunk_heads // 2
        i, at = t // per, t % per * lanes
        att_buf[y * groups + i, :, at : at + lanes] = joined.astype(jnp.bfloat16)
        if t % per == per - 1:
            att_copy(i, y).start()

    attend_pair(0)
    attend_pair(1)
    wo[0].serve(2)
    attend_pair(2)
    wo[0].cross(1)
    wo[1].serve(2)
    attend_pair(3)
    wo[1].cross(1)
    attend_pair(4)
    wo[2].serve(2)
    attend_pair(5)
    wo[2].cross(1)
    wo[3].serve(2)
    attend_pair(6)
    wo[3].cross(1)
    wo[0].serve(3)
    attend_pair(7)
    wo[1].serve(3)
    wo[0].cross(2)
    wo[2].serve(3)
    wo[1].cross(2)
    wo[3].serve(3)
    wo[0].cross(3)
    wo[1].cross(3)
    for item in [kvw] + wq:
        item.drain()
    whole = att_buf.at[pl.ds(0, groups)]
    remote(whole, whole, att_send, att_recv, {"blk": p.across + core}).wait_recv()

    def out_copy(k, j, here):
        return remote(out_buf.at[k, j], update_buf.at[y, k], out_send, out_recv.at[y, k],
                      {"blk": chip * 2 + j if here else p.across + j})

    for k in range(pieces):
        if k == pieces // 2:
            for late in wo[k:]:
                late.cross(2)
                late.cross(3)
        wo[k].settle()
        total = None
        for i in range(chips):
            product = jnp.dot(att_buf[i], wo_buf[k, i * 2 * rows_each : (i + 1) * 2 * rows_each, :], preferred_element_type=jnp.float32)
            total = product if total is None else total + product
        out_buf[k] = total.astype(jnp.bfloat16).reshape(2, cap, part)

        @pl.when(home_here)
        def _():
            update_buf[y, k] = out_buf[k, core]
            out_copy(k, 1 - core, True).start()

        @pl.when(away)
        def _():
            for j in range(2):
                out_copy(k, j, False).start()

    rows = final_ref[...].astype(jnp.float32)
    gate = jax.nn.sigmoid(jnp.sum(rows * router_ref[...].astype(jnp.float32).reshape(1, width), axis=1, keepdims=True))

    at_slot = lax.broadcasted_iota(jnp.int32, (tokens, cap), 0) == jnp.where(slot < count_ref[...], idx_ref[...], -1)
    put = at_slot.astype(jnp.float32)
    touched = jnp.max(put, axis=1, keepdims=True) > 0.0
    put = put.astype(jnp.bfloat16)

    def placed_copy(h, k):
        cols = slice(h * half + k * part, h * half + (k + 1) * part)
        return pltpu.make_async_copy(placed_buf.at[:, cols], out_ref.at[:, cols], placed_sem.at[h, k])

    def update_wait(h, k):
        remote(out_buf.at[k, 0], update_buf.at[h, k], out_send, out_recv.at[h, k], {"blk": p.across}).wait_recv()

    for k in range(pieces):
        update_wait(1 - y, k)

        @pl.when(away)
        def _():
            update_wait(y, k)

        for h in range(2):
            cols = slice(h * half + k * part, h * half + (k + 1) * part)
            done = (rows[:, cols] + gate * update_buf[h, k].astype(jnp.float32)).astype(jnp.bfloat16)
            placed = jnp.dot(put, done, preferred_element_type=jnp.float32)
            old = hidden_buf[:, cols].astype(jnp.float32)
            placed_buf[:, cols] = jnp.where(touched, placed, old).astype(jnp.bfloat16)
            placed_copy(h, k).start()

    for item in [kv, metas] + wo:
        item.drain()
    remote(whole, whole, att_send, att_recv, {"blk": p.across + core}).wait_send()
    rows_copy(1, core).wait_send()
    meta_copy(1, core).wait_send()

    def out_sent(homes):
        some = out_buf.at[:, pl.ds(0, homes)]
        remote(some, some, out_send, out_recv.at[0, 0], {"blk": p.across}).wait_send()

    @pl.when(home_here)
    def _():
        out_sent(1)

    @pl.when(away)
    def _():
        rows_copy(0, core).wait_send()
        meta_copy(0, core).wait_send()
        out_sent(2)

    for k in range(pieces):
        for h in range(2):
            placed_copy(h, k).wait()


def layer(n, keep, hidden, kept_idx, kept_count, router, norm_gain, qk_gain, query_weight, key_weight,
          value_weight, out_weight):
    tokens, width = hidden.shape
    cap = kept_idx.shape[1]
    pieces = 4
    lanes, chips, depth = 2 * HEAD, n // 2, n // 4
    half, slots = width // 2, 2 * cap
    part = half // pieces
    rows_each = query_weight.shape[0]
    half_size = HEAD // 2
    rates = rope_base ** (-(np.arange(half_size) * 2.0 / HEAD))
    rates = np.tile(rates, lanes // half_size)[None, :].astype(np.float32)
    dma = pltpu.SemaphoreType.DMA
    small = [
        kept_idx, kept_count.reshape(1, 1), norm_gain.reshape(1, width), router, key_weight, value_weight, qk_gain,
        jnp.asarray(rates),
    ]
    return pl.pallas_call(
        functools.partial(layer_kernel, n, pieces),
        out_shape=jax.ShapeDtypeStruct((tokens, width), jnp.bfloat16),
        in_specs=[HBM] * 11,
        out_specs=ANY,
        scratch_shapes=[pltpu.VMEM(a.shape, a.dtype) for a in small]
        + [
            dma((len(small),)),
            pltpu.VMEM((cap, width), jnp.bfloat16),
            pltpu.VMEM((tokens, width), jnp.bfloat16),
            dma((2, pieces)),
            pltpu.VMEM((cap, width), jnp.bfloat16),
            pltpu.VMEM((8, cap), jnp.int32),
            pltpu.VMEM((n, 8, cap), jnp.int32),
            pltpu.VMEM((2, cap, width), jnp.bfloat16),
            pltpu.VMEM((2, rows_each, lanes), jnp.bfloat16),
            pltpu.VMEM((width, lanes), jnp.bfloat16),
            pltpu.VMEM((pieces, width, part), jnp.bfloat16),
            pltpu.VMEM((pieces, width, part), jnp.bfloat16),
            pltpu.VMEM((half // HEAD, slots, lanes), jnp.bfloat16),
            pltpu.VMEM((slots, lanes), jnp.bfloat16),
            pltpu.VMEM((n * cap, lanes), jnp.bfloat16),
            pltpu.VMEM((keep, lanes), jnp.bfloat16),
            pltpu.VMEM((slots, keep), jnp.float32),
            pltpu.VMEM((chips, slots, width // chips), jnp.bfloat16),
            pltpu.VMEM((pieces, 2, cap, part), jnp.bfloat16),
            pltpu.VMEM((2, pieces, cap, part), jnp.bfloat16),
            pltpu.VMEM((slots, lanes), jnp.float32),
            pltpu.VMEM((slots, lanes), jnp.float32),
            dma((2,)), dma((2,)), dma((2,)), dma((2,)),
            dma(()), dma(()), dma(()), dma((2, pieces)),
            dma(()), dma(()), pltpu.VMEM((tokens, width), jnp.bfloat16),
        ]
        + Weight.semaphores(depth, 1 + 2 * pieces)
        + Line.semaphores(depth, 2),
        compiler_params=pltpu.CompilerParams(collective_id=1, has_side_effects=True),
    )(hidden, query_weight, out_weight, *small)


def body(
    n,
    hidden,
    kept_idx,
    kept_count,
    router,
    norm_gain,
    qk_gain,
    query_weight,
    key_weight,
    value_weight,
    out_weight,
):
    tokens = hidden.shape[0]
    cap = kept_idx.shape[1]
    keep = n * (tokens * KEEP_DEV // TOK_DEV)
    return layer(
        n, keep, hidden, kept_idx, kept_count, router, norm_gain, qk_gain, query_weight, key_weight,
        value_weight, out_weight,
    )


def attend(query_heads, query_ranks, key_block, value_block, key_ranks, state):
    prev_top, prev_total, prev_acc = state
    length = key_block.shape[0]
    keys_split = key_block.reshape(length, KV_HEADS, HEAD)
    values_split = value_block.reshape(length, KV_HEADS, HEAD)
    scores = jnp.einsum(
        "agch,bgh->gcab", query_heads, keys_split, preferred_element_type=jnp.float32
    ) * (1.0 / math.sqrt(HEAD))
    allowed = key_ranks[None, :] <= query_ranks[:, None]
    masked = jnp.where(allowed, scores, -1e30)
    new_top = jnp.maximum(prev_top, jnp.max(masked, axis=-1))
    weights = jnp.where(allowed, jnp.exp(masked - new_top[..., None]), 0.0)
    factor = jnp.exp(prev_top - new_top)
    new_total = prev_total * factor + jnp.sum(weights, axis=-1)
    new_acc = prev_acc * factor[..., None] + jnp.einsum(
        "gcab,bgh->gcah",
        weights.astype(jnp.bfloat16),
        values_split,
        preferred_element_type=jnp.float32,
    )
    return (new_top, new_total, new_acc)


def make_fold(query_heads, query_ranks, rank_of, state, pieces):
    key_piece, value_piece = pieces
    length = key_piece.shape[0]

    def inner(block_turn, inner_state):
        block_start = block_turn * 512
        key_block = lax.dynamic_slice_in_dim(key_piece, block_start, 512, 0)
        value_block = lax.dynamic_slice_in_dim(value_piece, block_start, 512, 0)
        key_ranks = rank_of(block_start + jnp.arange(512, dtype=jnp.int32))
        return attend(query_heads, query_ranks, key_block, value_block, key_ranks, inner_state)

    return lax.fori_loop(0, length // 512, inner, state)


def wide_body(
    hidden,
    kept_idx,
    kept_count,
    router,
    norm_gain,
    qk_gain,
    query_weight,
    key_weight,
    value_weight,
    out_weight,
):
    shard_count = lax.axis_size("blk")
    device = lax.axis_index("blk")
    width = hidden.shape[1]
    all_lists, all_counts = (
        lax.all_gather(kept_idx, "blk", axis=0, tiled=True),
        lax.all_gather(kept_count, "blk", axis=0, tiled=True),
    )
    starts = jnp.cumsum(all_counts) - all_counts
    own_start = starts[device]
    own_count = all_counts[device]
    list_slots = jnp.arange(CAP, dtype=jnp.int32)
    is_valid = list_slots < own_count
    token_rows = hidden[kept_idx[0]]
    gate_value = jax.nn.sigmoid(jnp.dot(token_rows, router, preferred_element_type=jnp.float32))
    slot_count = (CAP + shard_count - 1) // shard_count
    outgoing = jnp.where(is_valid[:, None], token_rows, jnp.zeros_like(token_rows))
    outgoing = jnp.roll(outgoing.reshape(slot_count, shard_count, width), own_start, axis=1)
    incoming = lax.all_to_all(outgoing, "blk", split_axis=1, concat_axis=1, tiled=True)
    query_ranks = device + jnp.arange(KEEP_DEV, dtype=jnp.int32) * shard_count
    source_ends = starts + all_counts
    source = jnp.sum((source_ends[None, :] <= query_ranks[:, None]).astype(jnp.int32), axis=1)
    within = query_ranks - starts[source]
    flat_index = within // shard_count * shard_count + source
    kept_rows = incoming.reshape(slot_count * shard_count, width)[flat_index]
    positions = source * TOK_DEV + all_lists[source, within]
    row_total = kept_rows.shape[0]
    normed = rms_scale(kept_rows.astype(jnp.float32), norm_gain).astype(jnp.bfloat16)
    query_cols = Q_HEADS * HEAD
    kv_cols = KV_HEADS * HEAD
    full_query, full_key, full_value, full_out = (
        lax.all_gather(query_weight, "blk", axis=0, tiled=True),
        lax.all_gather(key_weight, "blk", axis=0, tiled=True),
        lax.all_gather(value_weight, "blk", axis=0, tiled=True),
        lax.all_gather(out_weight, "blk", axis=0, tiled=True),
    )
    query_lin = jnp.dot(normed, full_query, preferred_element_type=jnp.float32)
    key_lin = jnp.dot(normed, full_key, preferred_element_type=jnp.float32)
    value_lin = jnp.dot(normed, full_value, preferred_element_type=jnp.float32)
    half_size = HEAD // 2
    rotation_rates = rope_base ** (-(jnp.arange(half_size, dtype=jnp.float32) * 2.0 / HEAD))
    angles = (positions.astype(jnp.float32)[:, None] * rotation_rates[None, :])[:, None, :]
    query_heads = rotate(
        rms_scale(query_lin.reshape(row_total, Q_HEADS, HEAD), qk_gain[0]), angles
    ).astype(jnp.bfloat16)
    key_heads = rotate(
        rms_scale(key_lin.reshape(row_total, KV_HEADS, HEAD), qk_gain[1]), angles
    ).astype(jnp.bfloat16)
    query_heads = query_heads.reshape(row_total, KV_HEADS, Q_HEADS // KV_HEADS, HEAD)
    key_flat = key_heads.reshape(row_total, kv_cols)
    value_flat = value_lin.astype(jnp.bfloat16)
    group_size = Q_HEADS // KV_HEADS
    start_state = (
        jnp.full((KV_HEADS, group_size, row_total), -1e30, jnp.float32),
        jnp.zeros((KV_HEADS, group_size, row_total), jnp.float32),
        jnp.zeros((KV_HEADS, group_size, row_total, HEAD), jnp.float32),
    )

    def strided_rank(slots_seen):
        return slots_seen // KEEP_DEV + slots_seen % KEEP_DEV * shard_count

    final_top, final_total, final_acc = make_fold(
        query_heads,
        query_ranks,
        strided_rank,
        start_state,
        (
            lax.all_gather(key_flat, "blk", axis=0, tiled=True),
            lax.all_gather(value_flat, "blk", axis=0, tiled=True),
        ),
    )
    attended = (
        (final_acc / final_total[..., None])
        .transpose(2, 0, 1, 3)
        .reshape(row_total, query_cols)
        .astype(jnp.bfloat16)
    )
    update = jnp.dot(attended, full_out, preferred_element_type=jnp.float32)
    update = update.astype(jnp.bfloat16)
    slot_grid = (
        jnp.arange(slot_count, dtype=jnp.int32)[:, None] * shard_count
        + jnp.mod(device - starts, shard_count)[None, :]
    )
    back_valid = slot_grid < all_counts[None, :]
    local_place = (starts[None, :] + slot_grid - device) // shard_count
    clipped = jnp.where(back_valid, local_place, 0)
    back_rows = jnp.where(back_valid[..., None], update[clipped], jnp.zeros((), jnp.bfloat16))
    returned = lax.all_to_all(back_rows, "blk", split_axis=1, concat_axis=1, tiled=True)
    returned = jnp.roll(returned, -own_start, axis=1).reshape(slot_count * shard_count, width)
    final = (
        token_rows.astype(jnp.float32) + gate_value[:, None] * returned.astype(jnp.float32)
    ).astype(jnp.bfloat16)
    target = jnp.where(is_valid, kept_idx[0], TOK_DEV)
    return hidden.at[target].set(final, mode="drop")


def solution(mesh):
    placed = (
        P(("groups", "blk"), None),
        P(("groups", "blk"), None),
        P(("groups", "blk")),
        P(),
        P(),
        P(),
        P("blk", None),
        P("blk", None),
        P("blk", None),
        P("blk", None),
    )
    n = mesh.shape["blk"]
    by_heads = n % 4 == 0 and Q_HEADS == 2 * n and mesh.shape["groups"] == KV_HEADS
    step = functools.partial(body, n) if by_heads else wide_body
    return jax.shard_map(
        step, mesh=mesh, in_specs=placed, out_specs=P(("groups", "blk"), None), check_vma=False
    )
```

```python
import functools
import math

import jax
import jax.numpy as jnp
import numpy as np
from jax import lax
from jax.experimental import pallas as pl
from jax.experimental.pallas import tpu as pltpu
from jax.sharding import PartitionSpec as P

Q_HEADS = 32
KV_HEADS = 2
HEAD = 64
TOK_DEV = 512
KEEP_DEV = 64
CAP = 128
MESH = pl.DeviceIdType.MESH
ANY = pl.BlockSpec(memory_space=pl.ANY)
HBM = pl.BlockSpec(memory_space=pltpu.HBM)


norm_eps = 1e-06
rope_base = 1000000.0


def rms_scale(values, scales):
    return values * lax.rsqrt(jnp.mean(values * values, axis=-1, keepdims=True) + norm_eps) * scales


def rotate(values, angles):
    half_size = values.shape[-1] // 2
    lower_half = values[..., :half_size]
    upper_half = values[..., half_size:]
    cosine = jnp.cos(angles)
    sine_part = jnp.sin(angles)
    return jnp.concatenate(
        [
            lower_half * cosine - upper_half * sine_part,
            upper_half * cosine + lower_half * sine_part,
        ],
        axis=-1,
    )


class Place:
    def __init__(self, n):
        self.depth = n // 4
        self.me = lax.axis_index("blk")
        self.group = lax.axis_index("groups")
        self.chip, self.core = self.me // 2, self.me % 2
        self.z, self.y = self.chip // 2, self.chip % 2
        self.partner = self.chip * 2 + 1 - self.core
        self.across = (self.chip + 1 - 2 * self.y) * 2

    def inside(self, z):
        return jnp.logical_and(z >= 0, z < self.depth)


def remote(source, target, send, recv, device):
    return pltpu.make_async_remote_copy(
        src_ref=source, dst_ref=target, send_sem=send, recv_sem=recv, device_id=device, device_id_type=MESH
    )


class Line:
    direct = True

    def __init__(self, place, own, buf, rows, view, sems):
        self.place, self.own, self.buf, self.rows, self.view = place, own, buf, rows, view
        self.z_send, self.z_recv, self.dup_send, self.dup_recv = sems
        self.dups = place.depth

    @staticmethod
    def semaphores(depth, count):
        dma = pltpu.SemaphoreType.DMA
        return [dma((count,)), dma((count, depth)), dma((count,)), dma((count,))]

    def along(self, source, z, offset):
        p = self.place
        return remote(source, self.view(z, p.core), self.z_send, self.z_recv.at[z], {"blk": p.me + 4 * offset})

    def dup(self, source, target):
        return remote(source, target, self.dup_send, self.dup_recv, {"blk": self.place.partner})

    def launch(self, source):
        p = self.place
        for offset in range(1, p.depth if self.direct else 2):
            for sign in (1, -1):
                @pl.when(p.inside(p.z + sign * offset))
                def _():
                    self.along(source, p.z, sign * offset).start()

    def start(self):
        p = self.place
        self.launch(self.own)
        self.dup(self.own, self.view(p.z, p.core)).start()

    def passed(self, z):
        pass

    def serve(self, distance):
        p = self.place
        for sign in (1, -1):
            z = p.z - sign * distance

            @pl.when(p.inside(z))
            def _():
                block = self.view(z, p.core)
                self.along(block, z, sign).wait_recv()
                if not self.direct:
                    @pl.when(p.inside(p.z + sign))
                    def _():
                        self.along(block, z, sign).start()

                self.passed(z)
                self.dup(block, block).start()

    def serve_all(self):
        for distance in range(1, self.place.depth):
            self.serve(distance)

    def total(self, blocks):
        return self.buf.at[pl.ds(0, blocks * self.rows)]

    def settle(self):
        whole = self.total(self.dups)
        self.dup(whole, whole).wait_recv()

    def drain(self):
        p = self.place

        def sent(blocks):
            whole = self.total(blocks)
            remote(whole, whole, self.z_send, self.z_recv.at[0], {"blk": p.partner}).wait_send()

        if self.direct:
            sent(p.depth - 1)
        else:
            middle = jnp.logical_and(p.z > 0, p.z < p.depth - 1)
            pl.when(middle)(lambda: sent(p.depth + 1))
            pl.when(jnp.logical_not(middle))(lambda: sent(1))
        whole = self.total(self.dups)
        self.dup(whole, whole).wait_send()


class Shared:
    def __init__(self, place, ref, buf, sems):
        self.place, self.ref, self.buf = place, ref, buf
        self.pieces, self.part = buf.shape[0], buf.shape[2]
        self.rows, self.half = ref.shape[0], self.pieces * buf.shape[2]
        self.per = self.pieces // 2
        self.z_send, self.z_recv, self.x_recv, self.side_send, self.side_recv, self.dup_send, self.dup_recv = sems

    @staticmethod
    def semaphores(depth, pieces, count):
        dma = pltpu.SemaphoreType.DMA
        return [dma((count,)), dma((count, pieces, depth)), dma((count, pieces, depth)), dma((count,)),
                dma((count, pieces)), dma((count,)), dma((count, pieces))]

    def columns(self, of, k):
        at = of * self.half + k * self.part
        return self.ref.at[:, pl.ds(pl.multiple_of(at, self.part), self.part)]

    def block(self, k, z, y, core):
        at = (4 * z + 2 * y + core) * self.rows
        return self.buf.at[k, pl.ds(pl.multiple_of(at, self.rows), self.rows)]

    def piece(self, unit, group):
        return self.per * group + unit % self.per

    def unit(self, unit, z, group):
        p = self.place
        return self.block(self.piece(unit, group), z, p.y if unit < self.per else 1 - p.y, p.core)

    def dup(self, k, source, target):
        return remote(source, target, self.dup_send, self.dup_recv.at[k], {"blk": self.place.partner})

    def side(self, k, y):
        p = self.place
        return remote(self.columns(1 - p.y, k), self.block(k, p.z, y, p.core), self.side_send, self.side_recv.at[k],
                      {"blk": p.across + p.core})

    def along(self, unit, source, z, sign):
        p = self.place
        return remote(source, self.unit(unit, z, p.group), self.z_send, self.z_recv.at[unit, z], {"blk": p.me + 4 * sign})

    def other(self, unit, z, group):
        block = self.unit(unit, z, group)
        return remote(block, block, self.side_send, self.x_recv.at[unit, z], {"groups": 1 - self.place.group})

    def start_side(self, group):
        for unit in range(self.per):
            self.side(self.piece(unit, group), self.place.y).start()

    def launch(self, unit, source):
        p = self.place
        for sign in (1, -1):
            @pl.when(p.inside(p.z + sign))
            def _():
                self.along(unit, source, p.z, sign).start()

    def start(self):
        p = self.place
        for unit in range(self.per):
            self.launch(unit, self.columns(p.y, self.piece(unit, p.group)))
        for k in range(self.pieces):
            self.dup(k, self.columns(p.y, k), self.block(k, p.z, p.y, p.core)).start()

    def keep(self, k, sem):
        p = self.place
        return pltpu.make_async_copy(self.columns(p.y, k), self.block(k, p.z, p.y, p.core), sem)

    def sided(self, unit, carried=True):
        p = self.place
        k = self.piece(unit, p.group if carried else 1 - p.group)
        block = self.block(k, p.z, 1 - p.y, p.core)
        self.side(k, 1 - p.y).wait_recv()
        if carried:
            self.launch(self.per + unit, block)
        self.dup(k, block, block).start()

    def serve(self, unit, distance):
        p = self.place
        for sign in (1, -1):
            z = p.z - sign * distance

            @pl.when(p.inside(z))
            def _():
                block = self.unit(unit, z, p.group)
                self.along(unit, block, z, sign).wait_recv()

                @pl.when(p.inside(p.z + sign))
                def _():
                    self.along(unit, block, z, sign).start()

                self.other(unit, z, p.group).start()
                self.dup(self.piece(unit, p.group), block, block).start()

    def cross(self, unit, distance):
        p = self.place
        for sign in (1, -1):
            z = p.z - sign * distance

            @pl.when(p.inside(z))
            def _():
                self.other(unit, z, 1 - p.group).wait_recv()
                block = self.unit(unit, z, 1 - p.group)
                self.dup(self.piece(unit, 1 - p.group), block, block).start()

    def settle(self, k):
        whole = self.buf.at[k, pl.ds(0, 2 * self.place.depth * self.rows)]
        self.dup(k, whole, whole).wait_recv()

    def drain(self):
        p = self.place

        def sent(sem, blocks):
            whole = self.buf.at[:, pl.ds(0, blocks * self.rows)]
            remote(whole, whole, sem, self.side_recv.at[0], {"blk": p.partner}).wait_send()

        middle = jnp.logical_and(p.z > 0, p.z < p.depth - 1)
        pl.when(middle)(lambda: sent(self.z_send, p.depth + 1))
        pl.when(jnp.logical_not(middle))(lambda: sent(self.z_send, 1))
        sent(self.side_send, p.depth)
        sent(self.dup_send, 2 * p.depth)


def turn(values, cosine, sine, lane):
    swapped = jnp.where(lane % HEAD < HEAD // 2, pltpu.roll(values, 2 * HEAD - HEAD // 2, 1), pltpu.roll(values, HEAD // 2, 1))
    return values * cosine + swapped * sine


def layer_kernel(n, pieces, hidden_ref, wq_ref, wo_ref, idx_hbm, count_hbm, norm_hbm, router_hbm, wk_hbm, wv_hbm,
                 gain_hbm, rate_hbm, out_ref, idx_ref, count_ref, norm_ref, router_ref, wk_ref, wv_ref, gain_ref, rate_ref,
                 small_sem, final_ref, placed_buf, placed_sem,
                 normed_buf, meta_buf, metas_buf, x_buf, kvw_own, kvw_buf, wq_buf, wo_buf, q_buf,
                 kv_own, kv_buf, pairs_buf, mask_buf, att_buf, out_buf, update_buf, cos_buf, sin_buf,
                 rows_send, rows_recv, meta_send, meta_recv, att_send, att_recv, out_send, out_recv, keep_sem, load_sem, hidden_buf, *sems):
    p = Place(n)
    depth, chip, core, y, me = p.depth, p.chip, p.core, p.y, p.me
    chips = n // 2
    barrier = pltpu.get_barrier_semaphore()
    for device in ({"blk": p.partner}, {"blk": p.across}, {"blk": p.across + 1}, {"groups": 1 - p.group}):
        pl.semaphore_signal(barrier, inc=1, device_id=device, device_id_type=MESH)
    for offset in range(1, depth):
        for sign in (1, -1):
            @pl.when(p.inside(p.z + sign * offset))
            def _():
                pl.semaphore_signal(barrier, inc=1, device_id={"blk": me + 4 * sign * offset}, device_id_type=MESH)
    load = pltpu.make_async_copy(hidden_ref, hidden_buf, load_sem)
    load.start()
    small = [pltpu.make_async_copy(source, target, small_sem.at[k]) for k, (source, target) in enumerate((
        (idx_hbm, idx_ref), (count_hbm, count_ref), (wk_hbm, wk_ref), (wv_hbm, wv_ref), (norm_hbm, norm_ref),
        (gain_hbm, gain_ref), (rate_hbm, rate_ref), (router_hbm, router_ref)))]
    for copy in small:
        copy.start()
    tokens, width = hidden_ref.shape
    cap = idx_ref.shape[1]
    lanes = 2 * HEAD
    half = width // 2
    part = half // pieces
    slots = 2 * cap
    keep = pairs_buf.shape[0]
    home_here = core == y
    away = jnp.logical_not(home_here)
    first_shard = 4 * p.z + 2 * core

    rows_each = wq_ref.shape[0]

    def take(sems, i):
        return [s.at[i] for s in sems]

    kvw_sems, a_sems, s_sems = sems[0], sems[1:5], sems[5:]
    def kvw_view(of):
        def view(z, at_core):
            at = (4 * z + 2 * of + at_core) * rows_each
            return kvw_buf.at[pl.ds(pl.multiple_of(at, rows_each), rows_each)]
        return view

    kvw_sources = (kvw_own.at[0], kvw_view(1 - y)(p.z, core))
    kvw_lines = [Line(p, source, kvw_buf, rows_each, kvw_view(of), take(a_sems, 2 + k))
                 for k, (source, of) in enumerate(zip(kvw_sources, (y, 1 - y)))]
    kvw_cross = remote(kvw_own.at[1], kvw_view(y)(p.z, core), kvw_sems.at[0], kvw_sems.at[1], {"blk": p.across + core})
    wq = Shared(p, wq_ref, wq_buf, take(s_sems, 0))
    wo = Shared(p, wo_ref, wo_buf, take(s_sems, 1))

    def pair_of(buf, each):
        def view(z, of):
            return buf.at[pl.ds(pl.multiple_of((4 * z + 2 * of) * each, 2 * each), 2 * each)]
        return view

    kv = Line(p, kv_own, kv_buf, slots, pair_of(kv_buf, cap), take(a_sems, 0))
    metas_view = pair_of(metas_buf, 1)
    metas = Line(p, metas_view(p.z, core), metas_buf, 2, metas_view, take(a_sems, 1))

    def worker(k):
        return {"blk": chip * 2 + y if k == 0 else p.across + y}

    def rows_copy(k, j):
        return remote(normed_buf, x_buf.at[j], rows_send.at[k], rows_recv.at[j], worker(k))

    def meta_copy(k, j):
        return remote(meta_buf, metas_buf.at[first_shard_of(k) + j], meta_send.at[k], meta_recv.at[j], worker(k))

    def first_shard_of(k):
        return 4 * p.z + 2 * y

    def meta_wait(k, j):
        return remote(meta_buf, metas_buf.at[first_shard + j], meta_send.at[k], meta_recv.at[j], worker(k))

    def arrived(copy):
        for j in range(2):
            @pl.when(jnp.logical_not(jnp.logical_and(home_here, core == j)))
            def _():
                copy(1, j).wait_recv()

    for item in (wq, wo):
        for k in range(pieces):
            item.keep(k, keep_sem).start()
    pl.semaphore_wait(barrier, 4 + depth - 1)
    wq.start_side(p.group)
    wq.start()
    for item in small:
        item.wait()
    def head_side(ref, of):
        return jnp.where(of == 0, ref[:, :HEAD].astype(jnp.float32), ref[:, HEAD:].astype(jnp.float32))

    for k, of in enumerate((y, 1 - y)):
        kvw_own[k] = jnp.concatenate([head_side(wk_ref, of), head_side(wv_ref, of)], axis=1).astype(jnp.bfloat16)
    line = lax.broadcasted_iota(jnp.int32, meta_buf.shape, 0)
    meta_buf[...] = jnp.where(line == 0, idx_ref[...], count_ref[...])

    kvw_cross.start()
    kvw_lines[0].start()
    meta_copy(1, core).start()

    @pl.when(home_here)
    def _():
        metas_buf[first_shard + core] = meta_buf[...]

    @pl.when(away)
    def _():
        meta_copy(0, core).start()

    load.wait()
    pick = lax.broadcasted_iota(jnp.int32, (tokens, cap), 0) == idx_ref[...]
    token_rows = lax.dot_general(
        pick.astype(jnp.float32).astype(jnp.bfloat16),
        hidden_buf[...],
        (((0,), (0,)), ((), ())),
        preferred_element_type=jnp.float32,
    )
    final_ref[...] = token_rows.astype(jnp.bfloat16)
    normed_buf[...] = rms_scale(token_rows, norm_ref[...]).astype(jnp.bfloat16)
    rows_copy(1, core).start()

    @pl.when(home_here)
    def _():
        x_buf[core] = normed_buf[...]

    @pl.when(away)
    def _():
        rows_copy(0, core).start()

    wo.start_side(p.group)
    wq.start_side(1 - p.group)
    wo.start_side(1 - p.group)
    wq.sided(0)
    wq.serve(0, 1)
    wq.sided(1)
    kvw_cross.wait_recv()
    kvw_lines[1].start()
    wq.serve(1, 1)
    wq.serve(2, 1)
    wq.serve(0, 2)
    wq.serve(3, 1)
    wq.serve(1, 2)
    arrived(meta_wait)
    metas.start()
    wq.serve(2, 2)
    wq.cross(0, 1)
    wq.serve(0, 3)
    wq.cross(1, 1)
    wq.serve(3, 2)
    wq.cross(2, 1)
    wq.cross(0, 2)
    wo.start()

    lane = lax.broadcasted_iota(jnp.int32, (1, lanes), 1)
    sign_row = jnp.where(lane % HEAD < HEAD // 2, -1.0, 1.0)
    square_row = lax.broadcasted_iota(jnp.int32, (cap, cap), 0)
    square_col = lax.broadcasted_iota(jnp.int32, (cap, cap), 1)
    slot = lax.broadcasted_iota(jnp.int32, (1, cap), 1)
    for j in range(2):
        spots = (metas_buf[first_shard + j, 0:1, :] + (first_shard + j) * tokens).astype(jnp.float32)
        spot = jnp.sum(jnp.where(square_row == square_col, spots, 0.0), axis=1, keepdims=True)
        angle = spot * rate_ref[...]
        cos_buf[j * cap : (j + 1) * cap, :] = jnp.cos(angle)
        sin_buf[j * cap : (j + 1) * cap, :] = jnp.sin(angle) * sign_row
    wq.cross(3, 1)
    metas.serve_all()
    for item in kvw_lines:
        item.serve_all()
    arrived(rows_copy)
    kept = wq_buf.at[0, pl.ds(0, 2 * pieces * rows_each)]
    pltpu.make_async_copy(kept, kept, keep_sem).wait()
    kvw_buf[pl.ds(pl.multiple_of(me * rows_each, rows_each), rows_each)] = kvw_own[0]
    for item in kvw_lines:
        item.settle()
    x_all = x_buf[...].reshape(slots, width)
    both = jnp.dot(x_all, kvw_buf[...], preferred_element_type=jnp.float32)
    gain = jnp.concatenate([gain_ref[1:2, :], gain_ref[1:2, :]], axis=1)
    mean = jnp.sum(jnp.where(lane < HEAD, both * both, 0.0), axis=1, keepdims=True) * (1.0 / HEAD)
    key = turn(both * lax.rsqrt(mean + norm_eps) * gain, cos_buf[...], sin_buf[...], lane)
    kv_own[...] = jnp.where(lane < HEAD, key, both).astype(jnp.bfloat16)
    kv.start()
    kv_buf[pl.ds(pl.multiple_of(first_shard * cap, slots), slots)] = kv_own[...]

    q_gain = jnp.concatenate([gain_ref[0:1, :], gain_ref[0:1, :]], axis=1) * (1.0 / math.sqrt(HEAD))

    def q_piece(k):
        wq.settle(k)
        lin = jnp.dot(x_buf[...].reshape(slots, width), wq_buf[k], preferred_element_type=jnp.float32)
        for t in range(part // lanes):
            total = lin[:, t * lanes : (t + 1) * lanes]
            squares = total * total
            first = jnp.sum(jnp.where(lane < HEAD, squares, 0.0), axis=1, keepdims=True)
            second = jnp.sum(jnp.where(lane < HEAD, 0.0, squares), axis=1, keepdims=True)
            mean = jnp.where(lane < HEAD, first, second) * (1.0 / HEAD)
            values = total * lax.rsqrt(mean + norm_eps) * q_gain
            values = turn(values, cos_buf[...], sin_buf[...], lane)
            h = 2 * (k * (part // lanes) + t)
            q_buf[h] = jnp.where(lane < HEAD, values, 0.0).astype(jnp.bfloat16)
            q_buf[h + 1] = jnp.where(lane < HEAD, pltpu.roll(values, HEAD, 1), 0.0).astype(jnp.bfloat16)

    wq.serve(1, 3)
    wq.serve(2, 3)
    wq.cross(1, 2)
    wq.serve(3, 3)
    wq.cross(2, 2)
    wo.sided(0)
    wq.cross(0, 3)
    wo.sided(1)
    wq.cross(3, 2)
    q_piece(wq.piece(0,p.group))
    wo.serve(0, 1)
    wq.cross(1, 3)
    q_piece(wq.piece(1,p.group))
    wo.serve(1, 1)
    wq.sided(0, False)
    wq.sided(1, False)
    wq.cross(2, 3)
    wq.cross(3, 3)
    metas.settle()
    starts, counts = [], []
    start = jnp.zeros((1, cap), jnp.int32)
    own_start = [jnp.zeros((1, cap), jnp.int32) for _ in range(2)]
    for s in range(n):
        count = metas_buf[s, 1:2, :]
        starts.append(start)
        counts.append(count)
        start = start + count
        for j in range(2):
            own_start[j] = own_start[j] + jnp.where(first_shard + j > s, count, 0)
    for j in range(2):
        for k in range(keep // cap):
            seen = square_col + k * cap - square_row <= own_start[j]
            mask_buf[j * cap : (j + 1) * cap, k * cap : (k + 1) * cap] = jnp.where(seen, 0.0, -1e30)

    q_piece(wq.piece(0,1-p.group))
    kv.serve_all()
    q_piece(wq.piece(1,1-p.group))
    wo.serve(2, 1)
    kv.settle()
    blocks = keep // cap
    for k in range(blocks):
        begin, end = k, min(n, k + n - blocks + 1)
        hits = []
        for s in range(begin, end):
            ranks = jnp.where(slot < counts[s], starts[s] + slot, -1)
            hits.append((square_row + k * cap == ranks).astype(jnp.float32).astype(jnp.bfloat16))
        dense = jnp.dot(jnp.concatenate(hits, axis=1), kv_buf[begin * cap : end * cap, :], preferred_element_type=jnp.float32)
        pairs_buf[k * cap : (k + 1) * cap, :] = dense.astype(jnp.bfloat16)

    def attend_head(h):
        scores = lax.dot_general(
            q_buf[h], pairs_buf[...], (((1,), (1,)), ((), ())), preferred_element_type=jnp.float32
        ) + mask_buf[...]
        top = jnp.max(scores, axis=-1, keepdims=True)
        weights = jnp.exp(scores - top)
        denominator = jnp.sum(weights, axis=-1, keepdims=True)
        mix = jnp.dot(weights.astype(jnp.bfloat16), pairs_buf[...], preferred_element_type=jnp.float32)
        return mix / denominator

    groups = chips // 2

    def att_copy(i, at, source):
        at = att_buf.at[source * groups + i, :, pl.ds(at, lanes)]
        return remote(at, at, att_send, att_recv, {"blk": p.across + core})

    heads = half // HEAD
    chunk_heads = heads // groups

    def attend_pair(t):
        mixes = [attend_head(2 * t + e) for e in range(2)]
        joined = jnp.where(lane < HEAD, pltpu.roll(mixes[0], HEAD, 1), mixes[1])
        per = chunk_heads // 2
        i, at = t // per, t % per * lanes
        att_buf[y * groups + i, :, at : at + lanes] = joined.astype(jnp.bfloat16)
        att_copy(i, at, y).start()

    attend_pair(0)
    wo.serve(3, 1)
    wo.serve(0, 2)
    attend_pair(1)
    wo.serve(2, 2)
    attend_pair(2)
    wo.serve(1, 2)
    wo.cross(0, 1)
    wo.sided(0, False)
    wo.sided(1, False)
    attend_pair(3)
    wo.serve(3, 2)
    wo.cross(1, 1)
    attend_pair(4)
    wo.cross(2, 1)
    wo.serve(0, 3)
    attend_pair(5)
    wo.serve(2, 3)
    wo.cross(0, 2)
    attend_pair(6)
    wo.serve(1, 3)
    wo.cross(3, 1)
    wo.cross(2, 2)
    attend_pair(7)
    wo.serve(3, 3)
    kvw_cross.wait_send()
    for item in (*kvw_lines, wq):
        item.drain()
    whole = att_buf.at[pl.ds(0, groups)]
    remote(whole, whole, att_send, att_recv, {"blk": p.across + core}).wait_recv()

    def out_copy(k, j, here):
        return remote(out_buf.at[k, j], update_buf.at[y, k], out_send, out_recv.at[y, k],
                      {"blk": chip * 2 + j if here else p.across + j})

    order = [wo.piece(unit, group) for group in (p.group, 1 - p.group) for unit in range(pieces // 2)]
    for i, k in enumerate(order):
        if i == 1:
            wo.cross(1, 2)
            wo.cross(3, 2)
            wo.cross(0, depth - 1)
            wo.cross(2, depth - 1)
        if i == 2:
            wo.cross(1, depth - 1)
            wo.cross(3, depth - 1)
        wo.settle(k)
        total = None
        for c in range(chips):
            product = jnp.dot(att_buf[c], wo_buf[k, c * 2 * rows_each : (c + 1) * 2 * rows_each, :], preferred_element_type=jnp.float32)
            total = product if total is None else total + product
        out_buf[k] = total.astype(jnp.bfloat16).reshape(2, cap, part)

        @pl.when(home_here)
        def _():
            update_buf[y, k] = out_buf[k, core]
            out_copy(k, 1 - core, True).start()

        @pl.when(away)
        def _():
            for j in range(2):
                out_copy(k, j, False).start()

    rows = final_ref[...].astype(jnp.float32)
    gate = jax.nn.sigmoid(jnp.sum(rows * router_ref[...].astype(jnp.float32).reshape(1, width), axis=1, keepdims=True))

    at_slot = lax.broadcasted_iota(jnp.int32, (tokens, cap), 0) == jnp.where(slot < count_ref[...], idx_ref[...], -1)
    put = at_slot.astype(jnp.float32)
    touched = jnp.max(put, axis=1, keepdims=True) > 0.0
    put = put.astype(jnp.bfloat16)

    def spot_of(h, k):
        return pl.ds(pl.multiple_of(h * half + k * part, part), part)

    def placed_copy(h, k):
        cols = spot_of(h, k)
        return pltpu.make_async_copy(placed_buf.at[:, cols], out_ref.at[:, cols], placed_sem.at[h, k])

    def update_wait(h, k):
        remote(out_buf.at[k, 0], update_buf.at[h, k], out_send, out_recv.at[h, k], {"blk": p.across}).wait_recv()

    for i, k in enumerate(order):
        update_wait(1 - y, k)

        @pl.when(away)
        def _():
            update_wait(y, k)

        for h in range(2):
            cols = spot_of(h, k)
            done = (final_ref[:, cols].astype(jnp.float32) + gate * update_buf[h, k].astype(jnp.float32)).astype(jnp.bfloat16)
            placed = jnp.dot(put, done, preferred_element_type=jnp.float32)
            old = hidden_buf[:, cols].astype(jnp.float32)
            placed_buf[:, cols] = jnp.where(touched, placed, old).astype(jnp.bfloat16)
            placed_copy(h, k).start()

    for item in (kv, metas, wo):
        item.drain()
    remote(whole, whole, att_send, att_recv, {"blk": p.across + core}).wait_send()
    rows_copy(1, core).wait_send()
    meta_copy(1, core).wait_send()

    def out_sent(homes):
        some = out_buf.at[:, pl.ds(0, homes)]
        remote(some, some, out_send, out_recv.at[0, 0], {"blk": p.across}).wait_send()

    @pl.when(home_here)
    def _():
        out_sent(1)

    @pl.when(away)
    def _():
        rows_copy(0, core).wait_send()
        meta_copy(0, core).wait_send()
        out_sent(2)

    for k in range(pieces):
        for h in range(2):
            placed_copy(h, k).wait()


def layer(n, keep, hidden, kept_idx, kept_count, router, norm_gain, qk_gain, query_weight, key_weight,
          value_weight, out_weight):
    tokens, width = hidden.shape
    cap = kept_idx.shape[1]
    pieces = 4
    lanes, chips, depth = 2 * HEAD, n // 2, n // 4
    half, slots = width // 2, 2 * cap
    part = half // pieces
    rows_each = query_weight.shape[0]
    half_size = HEAD // 2
    rates = rope_base ** (-(np.arange(half_size) * 2.0 / HEAD))
    rates = np.tile(rates, lanes // half_size)[None, :].astype(np.float32)
    dma = pltpu.SemaphoreType.DMA
    small = [
        kept_idx, kept_count.reshape(1, 1), norm_gain.reshape(1, width), router, key_weight, value_weight, qk_gain,
        jnp.asarray(rates),
    ]
    return pl.pallas_call(
        functools.partial(layer_kernel, n, pieces),
        out_shape=jax.ShapeDtypeStruct((tokens, width), jnp.bfloat16),
        in_specs=[HBM] * 11,
        out_specs=ANY,
        scratch_shapes=[pltpu.VMEM(a.shape, a.dtype) for a in small]
        + [
            dma((len(small),)),
            pltpu.VMEM((cap, width), jnp.bfloat16),
            pltpu.VMEM((tokens, width), jnp.bfloat16),
            dma((2, pieces)),
            pltpu.VMEM((cap, width), jnp.bfloat16),
            pltpu.VMEM((8, cap), jnp.int32),
            pltpu.VMEM((n, 8, cap), jnp.int32),
            pltpu.VMEM((2, cap, width), jnp.bfloat16),
            pltpu.VMEM((2, rows_each, lanes), jnp.bfloat16),
            pltpu.VMEM((width, lanes), jnp.bfloat16),
            pltpu.VMEM((pieces, width, part), jnp.bfloat16),
            pltpu.VMEM((pieces, width, part), jnp.bfloat16),
            pltpu.VMEM((half // HEAD, slots, lanes), jnp.bfloat16),
            pltpu.VMEM((slots, lanes), jnp.bfloat16),
            pltpu.VMEM((n * cap, lanes), jnp.bfloat16),
            pltpu.VMEM((keep, lanes), jnp.bfloat16),
            pltpu.VMEM((slots, keep), jnp.float32),
            pltpu.VMEM((chips, slots, width // chips), jnp.bfloat16),
            pltpu.VMEM((pieces, 2, cap, part), jnp.bfloat16),
            pltpu.VMEM((2, pieces, cap, part), jnp.bfloat16),
            pltpu.VMEM((slots, lanes), jnp.float32),
            pltpu.VMEM((slots, lanes), jnp.float32),
            dma((2,)), dma((2,)), dma((2,)), dma((2,)),
            dma(()), dma(()), dma(()), dma((2, pieces)),
            dma(()), dma(()), pltpu.VMEM((tokens, width), jnp.bfloat16),
        ]
        + [dma((2,))]
        + Line.semaphores(depth, 4)
        + Shared.semaphores(depth, pieces, 2),
        compiler_params=pltpu.CompilerParams(collective_id=1, has_side_effects=True),
    )(hidden, query_weight, out_weight, *small)


def body(
    n,
    hidden,
    kept_idx,
    kept_count,
    router,
    norm_gain,
    qk_gain,
    query_weight,
    key_weight,
    value_weight,
    out_weight,
):
    tokens = hidden.shape[0]
    cap = kept_idx.shape[1]
    keep = n * (tokens * KEEP_DEV // TOK_DEV)
    return layer(
        n, keep, hidden, kept_idx, kept_count, router, norm_gain, qk_gain, query_weight, key_weight,
        value_weight, out_weight,
    )


def attend(query_heads, query_ranks, key_block, value_block, key_ranks, state):
    prev_top, prev_total, prev_acc = state
    length = key_block.shape[0]
    keys_split = key_block.reshape(length, KV_HEADS, HEAD)
    values_split = value_block.reshape(length, KV_HEADS, HEAD)
    scores = jnp.einsum(
        "agch,bgh->gcab", query_heads, keys_split, preferred_element_type=jnp.float32
    ) * (1.0 / math.sqrt(HEAD))
    allowed = key_ranks[None, :] <= query_ranks[:, None]
    masked = jnp.where(allowed, scores, -1e30)
    new_top = jnp.maximum(prev_top, jnp.max(masked, axis=-1))
    weights = jnp.where(allowed, jnp.exp(masked - new_top[..., None]), 0.0)
    factor = jnp.exp(prev_top - new_top)
    new_total = prev_total * factor + jnp.sum(weights, axis=-1)
    new_acc = prev_acc * factor[..., None] + jnp.einsum(
        "gcab,bgh->gcah",
        weights.astype(jnp.bfloat16),
        values_split,
        preferred_element_type=jnp.float32,
    )
    return (new_top, new_total, new_acc)


def make_fold(query_heads, query_ranks, rank_of, state, pieces):
    key_piece, value_piece = pieces
    length = key_piece.shape[0]

    def inner(block_turn, inner_state):
        block_start = block_turn * 512
        key_block = lax.dynamic_slice_in_dim(key_piece, block_start, 512, 0)
        value_block = lax.dynamic_slice_in_dim(value_piece, block_start, 512, 0)
        key_ranks = rank_of(block_start + jnp.arange(512, dtype=jnp.int32))
        return attend(query_heads, query_ranks, key_block, value_block, key_ranks, inner_state)

    return lax.fori_loop(0, length // 512, inner, state)


def wide_body(
    hidden,
    kept_idx,
    kept_count,
    router,
    norm_gain,
    qk_gain,
    query_weight,
    key_weight,
    value_weight,
    out_weight,
):
    shard_count = lax.axis_size("blk")
    device = lax.axis_index("blk")
    width = hidden.shape[1]
    all_lists, all_counts = (
        lax.all_gather(kept_idx, "blk", axis=0, tiled=True),
        lax.all_gather(kept_count, "blk", axis=0, tiled=True),
    )
    starts = jnp.cumsum(all_counts) - all_counts
    own_start = starts[device]
    own_count = all_counts[device]
    list_slots = jnp.arange(CAP, dtype=jnp.int32)
    is_valid = list_slots < own_count
    token_rows = hidden[kept_idx[0]]
    gate_value = jax.nn.sigmoid(jnp.dot(token_rows, router, preferred_element_type=jnp.float32))
    slot_count = (CAP + shard_count - 1) // shard_count
    outgoing = jnp.where(is_valid[:, None], token_rows, jnp.zeros_like(token_rows))
    outgoing = jnp.roll(outgoing.reshape(slot_count, shard_count, width), own_start, axis=1)
    incoming = lax.all_to_all(outgoing, "blk", split_axis=1, concat_axis=1, tiled=True)
    query_ranks = device + jnp.arange(KEEP_DEV, dtype=jnp.int32) * shard_count
    source_ends = starts + all_counts
    source = jnp.sum((source_ends[None, :] <= query_ranks[:, None]).astype(jnp.int32), axis=1)
    within = query_ranks - starts[source]
    flat_index = within // shard_count * shard_count + source
    kept_rows = incoming.reshape(slot_count * shard_count, width)[flat_index]
    positions = source * TOK_DEV + all_lists[source, within]
    row_total = kept_rows.shape[0]
    normed = rms_scale(kept_rows.astype(jnp.float32), norm_gain).astype(jnp.bfloat16)
    query_cols = Q_HEADS * HEAD
    kv_cols = KV_HEADS * HEAD
    full_query, full_key, full_value, full_out = (
        lax.all_gather(query_weight, "blk", axis=0, tiled=True),
        lax.all_gather(key_weight, "blk", axis=0, tiled=True),
        lax.all_gather(value_weight, "blk", axis=0, tiled=True),
        lax.all_gather(out_weight, "blk", axis=0, tiled=True),
    )
    query_lin = jnp.dot(normed, full_query, preferred_element_type=jnp.float32)
    key_lin = jnp.dot(normed, full_key, preferred_element_type=jnp.float32)
    value_lin = jnp.dot(normed, full_value, preferred_element_type=jnp.float32)
    half_size = HEAD // 2
    rotation_rates = rope_base ** (-(jnp.arange(half_size, dtype=jnp.float32) * 2.0 / HEAD))
    angles = (positions.astype(jnp.float32)[:, None] * rotation_rates[None, :])[:, None, :]
    query_heads = rotate(
        rms_scale(query_lin.reshape(row_total, Q_HEADS, HEAD), qk_gain[0]), angles
    ).astype(jnp.bfloat16)
    key_heads = rotate(
        rms_scale(key_lin.reshape(row_total, KV_HEADS, HEAD), qk_gain[1]), angles
    ).astype(jnp.bfloat16)
    query_heads = query_heads.reshape(row_total, KV_HEADS, Q_HEADS // KV_HEADS, HEAD)
    key_flat = key_heads.reshape(row_total, kv_cols)
    value_flat = value_lin.astype(jnp.bfloat16)
    group_size = Q_HEADS // KV_HEADS
    start_state = (
        jnp.full((KV_HEADS, group_size, row_total), -1e30, jnp.float32),
        jnp.zeros((KV_HEADS, group_size, row_total), jnp.float32),
        jnp.zeros((KV_HEADS, group_size, row_total, HEAD), jnp.float32),
    )

    def strided_rank(slots_seen):
        return slots_seen // KEEP_DEV + slots_seen % KEEP_DEV * shard_count

    final_top, final_total, final_acc = make_fold(
        query_heads,
        query_ranks,
        strided_rank,
        start_state,
        (
            lax.all_gather(key_flat, "blk", axis=0, tiled=True),
            lax.all_gather(value_flat, "blk", axis=0, tiled=True),
        ),
    )
    attended = (
        (final_acc / final_total[..., None])
        .transpose(2, 0, 1, 3)
        .reshape(row_total, query_cols)
        .astype(jnp.bfloat16)
    )
    update = jnp.dot(attended, full_out, preferred_element_type=jnp.float32)
    update = update.astype(jnp.bfloat16)
    slot_grid = (
        jnp.arange(slot_count, dtype=jnp.int32)[:, None] * shard_count
        + jnp.mod(device - starts, shard_count)[None, :]
    )
    back_valid = slot_grid < all_counts[None, :]
    local_place = (starts[None, :] + slot_grid - device) // shard_count
    clipped = jnp.where(back_valid, local_place, 0)
    back_rows = jnp.where(back_valid[..., None], update[clipped], jnp.zeros((), jnp.bfloat16))
    returned = lax.all_to_all(back_rows, "blk", split_axis=1, concat_axis=1, tiled=True)
    returned = jnp.roll(returned, -own_start, axis=1).reshape(slot_count * shard_count, width)
    final = (
        token_rows.astype(jnp.float32) + gate_value[:, None] * returned.astype(jnp.float32)
    ).astype(jnp.bfloat16)
    target = jnp.where(is_valid, kept_idx[0], TOK_DEV)
    return hidden.at[target].set(final, mode="drop")


def solution(mesh):
    placed = (
        P(("groups", "blk"), None),
        P(("groups", "blk"), None),
        P(("groups", "blk")),
        P(),
        P(),
        P(),
        P("blk", None),
        P("blk", None),
        P("blk", None),
        P("blk", None),
    )
    n = mesh.shape["blk"]
    by_heads = n % 4 == 0 and Q_HEADS == 2 * n and mesh.shape["groups"] == KV_HEADS
    step = functools.partial(body, n) if by_heads else wide_body
    return jax.shard_map(
        step, mesh=mesh, in_specs=placed, out_specs=P(("groups", "blk"), None), check_vma=False
    )
```

```python
import functools
import math

import jax
import jax.numpy as jnp
import numpy as np
from jax import lax
from jax.experimental import pallas as pl
from jax.experimental.pallas import tpu as pltpu
from jax.sharding import PartitionSpec as P

Q_HEADS = 32
KV_HEADS = 2
HEAD = 64
TOK_DEV = 512
KEEP_DEV = 64
CAP = 128
MESH = pl.DeviceIdType.MESH
ANY = pl.BlockSpec(memory_space=pl.ANY)
HBM = pl.BlockSpec(memory_space=pltpu.HBM)


norm_eps = 1e-06
rope_base = 1000000.0


def rms_scale(values, scales):
    return values * lax.rsqrt(jnp.mean(values * values, axis=-1, keepdims=True) + norm_eps) * scales


def rotate(values, angles):
    half_size = values.shape[-1] // 2
    lower_half = values[..., :half_size]
    upper_half = values[..., half_size:]
    cosine = jnp.cos(angles)
    sine_part = jnp.sin(angles)
    return jnp.concatenate(
        [
            lower_half * cosine - upper_half * sine_part,
            upper_half * cosine + lower_half * sine_part,
        ],
        axis=-1,
    )


class Place:
    def __init__(self, n):
        self.depth = n // 4
        self.me = lax.axis_index("blk")
        self.group = lax.axis_index("groups")
        self.chip, self.core = self.me // 2, self.me % 2
        self.z, self.y = self.chip // 2, self.chip % 2
        self.partner = self.chip * 2 + 1 - self.core
        self.across = (self.chip + 1 - 2 * self.y) * 2

    def inside(self, z):
        return jnp.logical_and(z >= 0, z < self.depth)


def remote(source, target, send, recv, device):
    return pltpu.make_async_remote_copy(
        src_ref=source, dst_ref=target, send_sem=send, recv_sem=recv, device_id=device, device_id_type=MESH
    )


class Line:
    direct = True

    def __init__(self, place, own, buf, rows, view, sems):
        self.place, self.own, self.buf, self.rows, self.view = place, own, buf, rows, view
        self.z_send, self.z_recv, self.dup_send, self.dup_recv = sems
        self.dups = place.depth

    @staticmethod
    def semaphores(depth, count):
        dma = pltpu.SemaphoreType.DMA
        return [dma((count,)), dma((count, depth)), dma((count,)), dma((count,))]

    def along(self, source, z, offset):
        p = self.place
        return remote(source, self.view(z, p.core), self.z_send, self.z_recv.at[z], {"blk": p.me + 4 * offset})

    def dup(self, source, target):
        return remote(source, target, self.dup_send, self.dup_recv, {"blk": self.place.partner})

    def launch(self, source):
        p = self.place
        for offset in range(1, p.depth if self.direct else 2):
            for sign in (1, -1):
                @pl.when(p.inside(p.z + sign * offset))
                def _():
                    self.along(source, p.z, sign * offset).start()

    def start(self):
        p = self.place
        self.launch(self.own)
        self.dup(self.own, self.view(p.z, p.core)).start()

    def passed(self, z):
        pass

    def serve(self, distance):
        p = self.place
        for sign in (1, -1):
            z = p.z - sign * distance

            @pl.when(p.inside(z))
            def _():
                block = self.view(z, p.core)
                self.along(block, z, sign).wait_recv()
                if not self.direct:
                    @pl.when(p.inside(p.z + sign))
                    def _():
                        self.along(block, z, sign).start()

                self.passed(z)
                self.dup(block, block).start()

    def serve_all(self):
        for distance in range(1, self.place.depth):
            self.serve(distance)

    def total(self, blocks):
        return self.buf.at[pl.ds(0, blocks * self.rows)]

    def settle(self):
        whole = self.total(self.dups)
        self.dup(whole, whole).wait_recv()

    def drain(self):
        p = self.place

        def sent(blocks):
            whole = self.total(blocks)
            remote(whole, whole, self.z_send, self.z_recv.at[0], {"blk": p.partner}).wait_send()

        if self.direct:
            sent(p.depth - 1)
        else:
            middle = jnp.logical_and(p.z > 0, p.z < p.depth - 1)
            pl.when(middle)(lambda: sent(p.depth + 1))
            pl.when(jnp.logical_not(middle))(lambda: sent(1))
        whole = self.total(self.dups)
        self.dup(whole, whole).wait_send()


class Shared:
    def __init__(self, place, ref, buf, sems):
        self.place, self.ref, self.buf = place, ref, buf
        self.pieces, self.part = buf.shape[0], buf.shape[2]
        self.rows, self.half = ref.shape[0], self.pieces * buf.shape[2]
        self.per = self.pieces // 2
        self.z_send, self.z_recv, self.x_recv, self.side_send, self.side_recv, self.dup_send, self.dup_recv = sems

    @staticmethod
    def semaphores(depth, pieces, count):
        dma = pltpu.SemaphoreType.DMA
        return [dma((count,)), dma((count, pieces, depth)), dma((count, pieces, depth)), dma((count,)),
                dma((count, pieces)), dma((count,)), dma((count, pieces))]

    def columns(self, of, k):
        at = of * self.half + k * self.part
        return self.ref.at[:, pl.ds(pl.multiple_of(at, self.part), self.part)]

    def block(self, k, z, y, core):
        at = (4 * z + 2 * y + core) * self.rows
        return self.buf.at[k, pl.ds(pl.multiple_of(at, self.rows), self.rows)]

    def piece(self, unit, group):
        return self.per * group + unit % self.per

    def unit(self, unit, z, group):
        p = self.place
        return self.block(self.piece(unit, group), z, p.y if unit < self.per else 1 - p.y, p.core)

    def dup(self, k, source, target):
        return remote(source, target, self.dup_send, self.dup_recv.at[k], {"blk": self.place.partner})

    def side(self, k, y):
        p = self.place
        return remote(self.columns(1 - p.y, k), self.block(k, p.z, y, p.core), self.side_send, self.side_recv.at[k],
                      {"blk": p.across + p.core})

    def along(self, unit, source, z, sign):
        p = self.place
        return remote(source, self.unit(unit, z, p.group), self.z_send, self.z_recv.at[unit, z], {"blk": p.me + 4 * sign})

    def other(self, unit, z, group):
        block = self.unit(unit, z, group)
        return remote(block, block, self.side_send, self.x_recv.at[unit, z], {"groups": 1 - self.place.group})

    def start_side(self, group):
        for unit in range(self.per):
            self.side(self.piece(unit, group), self.place.y).start()

    def launch(self, unit, source):
        p = self.place
        for sign in (1, -1):
            @pl.when(p.inside(p.z + sign))
            def _():
                self.along(unit, source, p.z, sign).start()

    def start(self):
        p = self.place
        for unit in range(self.per):
            self.launch(unit, self.columns(p.y, self.piece(unit, p.group)))
        for k in range(self.pieces):
            self.dup(k, self.columns(p.y, k), self.block(k, p.z, p.y, p.core)).start()

    def keep(self, k, sem):
        p = self.place
        return pltpu.make_async_copy(self.columns(p.y, k), self.block(k, p.z, p.y, p.core), sem)

    def sided(self, unit, carried=True):
        p = self.place
        k = self.piece(unit, p.group if carried else 1 - p.group)
        block = self.block(k, p.z, 1 - p.y, p.core)
        self.side(k, 1 - p.y).wait_recv()
        if carried:
            self.launch(self.per + unit, block)
        self.dup(k, block, block).start()

    def serve(self, unit, distance):
        p = self.place
        for sign in (1, -1):
            z = p.z - sign * distance

            @pl.when(p.inside(z))
            def _():
                block = self.unit(unit, z, p.group)
                self.along(unit, block, z, sign).wait_recv()

                @pl.when(p.inside(p.z + sign))
                def _():
                    self.along(unit, block, z, sign).start()

                self.other(unit, z, p.group).start()
                self.dup(self.piece(unit, p.group), block, block).start()

    def cross(self, unit, distance):
        p = self.place
        for sign in (1, -1):
            z = p.z - sign * distance

            @pl.when(p.inside(z))
            def _():
                self.other(unit, z, 1 - p.group).wait_recv()
                block = self.unit(unit, z, 1 - p.group)
                self.dup(self.piece(unit, 1 - p.group), block, block).start()

    def settle(self, k):
        whole = self.buf.at[k, pl.ds(0, 2 * self.place.depth * self.rows)]
        self.dup(k, whole, whole).wait_recv()

    def drain(self):
        p = self.place

        def sent(sem, blocks):
            whole = self.buf.at[:, pl.ds(0, blocks * self.rows)]
            remote(whole, whole, sem, self.side_recv.at[0], {"blk": p.partner}).wait_send()

        middle = jnp.logical_and(p.z > 0, p.z < p.depth - 1)
        pl.when(middle)(lambda: sent(self.z_send, p.depth + 1))
        pl.when(jnp.logical_not(middle))(lambda: sent(self.z_send, 1))
        sent(self.side_send, p.depth)
        sent(self.dup_send, 2 * p.depth)


def turn(values, cosine, sine, lane):
    swapped = jnp.where(lane % HEAD < HEAD // 2, pltpu.roll(values, 2 * HEAD - HEAD // 2, 1), pltpu.roll(values, HEAD // 2, 1))
    return values * cosine + swapped * sine


def layer_kernel(n, pieces, hidden_ref, wq_ref, wo_ref, idx_hbm, count_hbm, norm_hbm, router_hbm, wk_hbm, wv_hbm,
                 gain_hbm, rate_hbm, out_ref, idx_ref, count_ref, norm_ref, router_ref, wk_ref, wv_ref, gain_ref, rate_ref,
                 small_sem, final_ref, placed_buf, placed_sem,
                 normed_buf, meta_buf, metas_buf, x_buf, kvw_own, kvw_buf, wq_buf, wo_buf, q_buf,
                 kv_own, kv_buf, pairs_buf, mask_buf, att_buf, out_buf, update_buf, cos_buf, sin_buf,
                 rows_send, rows_recv, meta_send, meta_recv, att_send, att_recv, out_send, out_recv, keep_sem, load_sem, hidden_buf, *sems):
    p = Place(n)
    depth, chip, core, y, me = p.depth, p.chip, p.core, p.y, p.me
    chips = n // 2
    barrier = pltpu.get_barrier_semaphore()
    for device in ({"blk": p.partner}, {"blk": p.across}, {"blk": p.across + 1}, {"groups": 1 - p.group}):
        pl.semaphore_signal(barrier, inc=1, device_id=device, device_id_type=MESH)
    for offset in range(1, depth):
        for sign in (1, -1):
            @pl.when(p.inside(p.z + sign * offset))
            def _():
                pl.semaphore_signal(barrier, inc=1, device_id={"blk": me + 4 * sign * offset}, device_id_type=MESH)
    load = pltpu.make_async_copy(hidden_ref, hidden_buf, load_sem)
    load.start()
    small = [pltpu.make_async_copy(source, target, small_sem.at[k]) for k, (source, target) in enumerate((
        (idx_hbm, idx_ref), (count_hbm, count_ref), (wk_hbm, wk_ref), (wv_hbm, wv_ref), (norm_hbm, norm_ref),
        (gain_hbm, gain_ref), (rate_hbm, rate_ref), (router_hbm, router_ref)))]
    for copy in small:
        copy.start()
    tokens, width = hidden_ref.shape
    cap = idx_ref.shape[1]
    lanes = 2 * HEAD
    half = width // 2
    part = half // pieces
    slots = 2 * cap
    keep = pairs_buf.shape[0]
    home_here = core == y
    away = jnp.logical_not(home_here)
    first_shard = 4 * p.z + 2 * core

    rows_each = wq_ref.shape[0]

    def take(sems, i):
        return [s.at[i] for s in sems]

    kvw_sems, a_sems, s_sems = sems[0], sems[1:5], sems[5:]
    def kvw_view(of):
        def view(z, at_core):
            at = (4 * z + 2 * of + at_core) * rows_each
            return kvw_buf.at[pl.ds(pl.multiple_of(at, rows_each), rows_each)]
        return view

    kvw_sources = (kvw_own.at[0], kvw_view(1 - y)(p.z, core))
    kvw_lines = [Line(p, source, kvw_buf, rows_each, kvw_view(of), take(a_sems, 2 + k))
                 for k, (source, of) in enumerate(zip(kvw_sources, (y, 1 - y)))]
    kvw_cross = remote(kvw_own.at[1], kvw_view(y)(p.z, core), kvw_sems.at[0], kvw_sems.at[1], {"blk": p.across + core})
    wq = Shared(p, wq_ref, wq_buf, take(s_sems, 0))
    wo = Shared(p, wo_ref, wo_buf, take(s_sems, 1))

    def pair_of(buf, each):
        def view(z, of):
            return buf.at[pl.ds(pl.multiple_of((4 * z + 2 * of) * each, 2 * each), 2 * each)]
        return view

    kv = Line(p, kv_own, kv_buf, slots, pair_of(kv_buf, cap), take(a_sems, 0))
    metas_view = pair_of(metas_buf, 1)
    metas = Line(p, metas_view(p.z, core), metas_buf, 2, metas_view, take(a_sems, 1))

    def worker(k):
        return {"blk": chip * 2 + y if k == 0 else p.across + y}

    def rows_copy(k, j):
        return remote(normed_buf, x_buf.at[j], rows_send.at[k], rows_recv.at[j], worker(k))

    def meta_copy(k, j):
        return remote(meta_buf, metas_buf.at[first_shard_of(k) + j], meta_send.at[k], meta_recv.at[j], worker(k))

    def first_shard_of(k):
        return 4 * p.z + 2 * y

    def meta_wait(k, j):
        return remote(meta_buf, metas_buf.at[first_shard + j], meta_send.at[k], meta_recv.at[j], worker(k))

    def arrived(copy):
        for j in range(2):
            @pl.when(jnp.logical_not(jnp.logical_and(home_here, core == j)))
            def _():
                copy(1, j).wait_recv()

    for item in (wq, wo):
        for k in range(pieces):
            item.keep(k, keep_sem).start()
    pl.semaphore_wait(barrier, 4 + depth - 1)
    wq.start_side(p.group)
    wq.start()
    for item in small:
        item.wait()
    def head_side(ref, of):
        return jnp.where(of == 0, ref[:, :HEAD].astype(jnp.float32), ref[:, HEAD:].astype(jnp.float32))

    for k, of in enumerate((y, 1 - y)):
        kvw_own[k] = jnp.concatenate([head_side(wk_ref, of), head_side(wv_ref, of)], axis=1).astype(jnp.bfloat16)
    line = lax.broadcasted_iota(jnp.int32, meta_buf.shape, 0)
    meta_buf[...] = jnp.where(line == 0, idx_ref[...], count_ref[...])

    kvw_cross.start()
    kvw_lines[0].start()
    meta_copy(1, core).start()

    @pl.when(home_here)
    def _():
        metas_buf[first_shard + core] = meta_buf[...]

    @pl.when(away)
    def _():
        meta_copy(0, core).start()

    load.wait()
    pick = lax.broadcasted_iota(jnp.int32, (tokens, cap), 0) == idx_ref[...]
    token_rows = lax.dot_general(
        pick.astype(jnp.float32).astype(jnp.bfloat16),
        hidden_buf[...],
        (((0,), (0,)), ((), ())),
        preferred_element_type=jnp.float32,
    )
    final_ref[...] = token_rows.astype(jnp.bfloat16)
    normed_buf[...] = rms_scale(token_rows, norm_ref[...]).astype(jnp.bfloat16)
    rows_copy(1, core).start()

    @pl.when(home_here)
    def _():
        x_buf[core] = normed_buf[...]

    @pl.when(away)
    def _():
        rows_copy(0, core).start()

    wo.start_side(p.group)
    wq.start_side(1 - p.group)
    wo.start_side(1 - p.group)
    wq.sided(0)
    wq.serve(0, 1)
    wq.sided(1)
    kvw_cross.wait_recv()
    kvw_lines[1].start()
    wq.serve(1, 1)
    wq.serve(2, 1)
    arrived(meta_wait)
    metas.start()
    wq.serve(0, 2)
    wq.serve(3, 1)
    wq.serve(1, 2)
    wq.serve(2, 2)
    for item in kvw_lines:
        item.serve_all()
    wq.cross(0, 1)
    wq.serve(0, 3)
    wq.cross(1, 1)
    wq.serve(3, 2)
    wo.start()

    lane = lax.broadcasted_iota(jnp.int32, (1, lanes), 1)
    sign_row = jnp.where(lane % HEAD < HEAD // 2, -1.0, 1.0)
    square_row = lax.broadcasted_iota(jnp.int32, (cap, cap), 0)
    square_col = lax.broadcasted_iota(jnp.int32, (cap, cap), 1)
    slot = lax.broadcasted_iota(jnp.int32, (1, cap), 1)
    for j in range(2):
        spots = (metas_buf[first_shard + j, 0:1, :] + (first_shard + j) * tokens).astype(jnp.float32)
        spot = jnp.sum(jnp.where(square_row == square_col, spots, 0.0), axis=1, keepdims=True)
        angle = spot * rate_ref[...]
        cos_buf[j * cap : (j + 1) * cap, :] = jnp.cos(angle)
        sin_buf[j * cap : (j + 1) * cap, :] = jnp.sin(angle) * sign_row
    arrived(rows_copy)
    kept = wq_buf.at[0, pl.ds(0, 2 * pieces * rows_each)]
    pltpu.make_async_copy(kept, kept, keep_sem).wait()
    kvw_buf[pl.ds(pl.multiple_of(me * rows_each, rows_each), rows_each)] = kvw_own[0]
    for item in kvw_lines:
        item.settle()
    x_all = x_buf[...].reshape(slots, width)
    both = jnp.dot(x_all, kvw_buf[...], preferred_element_type=jnp.float32)
    gain = jnp.concatenate([gain_ref[1:2, :], gain_ref[1:2, :]], axis=1)
    mean = jnp.sum(jnp.where(lane < HEAD, both * both, 0.0), axis=1, keepdims=True) * (1.0 / HEAD)
    key = turn(both * lax.rsqrt(mean + norm_eps) * gain, cos_buf[...], sin_buf[...], lane)
    kv_own[...] = jnp.where(lane < HEAD, key, both).astype(jnp.bfloat16)
    kv.start()
    kv_buf[pl.ds(pl.multiple_of(first_shard * cap, slots), slots)] = kv_own[...]

    q_gain = jnp.concatenate([gain_ref[0:1, :], gain_ref[0:1, :]], axis=1) * (1.0 / math.sqrt(HEAD))

    def q_piece(k):
        wq.settle(k)
        lin = jnp.dot(x_buf[...].reshape(slots, width), wq_buf[k], preferred_element_type=jnp.float32)
        for t in range(part // lanes):
            total = lin[:, t * lanes : (t + 1) * lanes]
            squares = total * total
            first = jnp.sum(jnp.where(lane < HEAD, squares, 0.0), axis=1, keepdims=True)
            second = jnp.sum(jnp.where(lane < HEAD, 0.0, squares), axis=1, keepdims=True)
            mean = jnp.where(lane < HEAD, first, second) * (1.0 / HEAD)
            values = total * lax.rsqrt(mean + norm_eps) * q_gain
            values = turn(values, cos_buf[...], sin_buf[...], lane)
            h = 2 * (k * (part // lanes) + t)
            q_buf[h] = jnp.where(lane < HEAD, values, 0.0).astype(jnp.bfloat16)
            q_buf[h + 1] = jnp.where(lane < HEAD, pltpu.roll(values, HEAD, 1), 0.0).astype(jnp.bfloat16)

    wq.serve(1, 3)
    wq.cross(2, 1)
    wq.cross(0, 2)
    wq.cross(3, 1)
    wq.serve(2, 3)
    wq.cross(1, 2)
    wq.serve(3, 3)
    wq.cross(2, 2)
    wo.sided(0)
    wq.cross(0, 3)
    wo.sided(1)
    wq.cross(3, 2)
    metas.serve_all()
    q_piece(wq.piece(0,p.group))
    wo.serve(0, 1)
    wq.cross(1, 3)
    q_piece(wq.piece(1,p.group))
    wq.sided(0, False)
    wq.sided(1, False)
    wq.cross(2, 3)
    wq.cross(3, 3)
    metas.settle()
    starts, counts = [], []
    start = jnp.zeros((1, cap), jnp.int32)
    own_start = [jnp.zeros((1, cap), jnp.int32) for _ in range(2)]
    for s in range(n):
        count = metas_buf[s, 1:2, :]
        starts.append(start)
        counts.append(count)
        start = start + count
        for j in range(2):
            own_start[j] = own_start[j] + jnp.where(first_shard + j > s, count, 0)
    for j in range(2):
        for k in range(keep // cap):
            seen = square_col + k * cap - square_row <= own_start[j]
            mask_buf[j * cap : (j + 1) * cap, k * cap : (k + 1) * cap] = jnp.where(seen, 0.0, -1e30)

    q_piece(wq.piece(0,1-p.group))
    wo.serve(1, 1)
    kv.serve_all()
    q_piece(wq.piece(1,1-p.group))
    kv.settle()
    blocks = keep // cap
    for k in range(blocks):
        begin, end = k, min(n, k + n - blocks + 1)
        hits = []
        for s in range(begin, end):
            ranks = jnp.where(slot < counts[s], starts[s] + slot, -1)
            hits.append((square_row + k * cap == ranks).astype(jnp.float32).astype(jnp.bfloat16))
        dense = jnp.dot(jnp.concatenate(hits, axis=1), kv_buf[begin * cap : end * cap, :], preferred_element_type=jnp.float32)
        pairs_buf[k * cap : (k + 1) * cap, :] = dense.astype(jnp.bfloat16)

    def attend_head(h):
        scores = lax.dot_general(
            q_buf[h], pairs_buf[...], (((1,), (1,)), ((), ())), preferred_element_type=jnp.float32
        ) + mask_buf[...]
        top = jnp.max(scores, axis=-1, keepdims=True)
        weights = jnp.exp(scores - top)
        denominator = jnp.sum(weights, axis=-1, keepdims=True)
        mix = jnp.dot(weights.astype(jnp.bfloat16), pairs_buf[...], preferred_element_type=jnp.float32)
        return mix / denominator

    groups = chips // 2

    def att_copy(i, at, source):
        at = att_buf.at[source * groups + i, :, pl.ds(at, lanes)]
        return remote(at, at, att_send, att_recv, {"blk": p.across + core})

    heads = half // HEAD
    chunk_heads = heads // groups

    def attend_pair(t):
        mixes = [attend_head(2 * t + e) for e in range(2)]
        joined = jnp.where(lane < HEAD, pltpu.roll(mixes[0], HEAD, 1), mixes[1])
        per = chunk_heads // 2
        i, at = t // per, t % per * lanes
        att_buf[y * groups + i, :, at : at + lanes] = joined.astype(jnp.bfloat16)
        att_copy(i, at, y).start()

    attend_pair(0)
    wo.serve(2, 1)
    wo.serve(3, 1)
    attend_pair(1)
    wo.serve(0, 2)
    attend_pair(2)
    wo.cross(0, 1)
    attend_pair(3)
    wo.serve(2, 2)
    wo.sided(0, False)
    wo.sided(1, False)
    wo.cross(1, 1)
    attend_pair(4)
    wo.serve(1, 2)
    wo.cross(2, 1)
    attend_pair(5)
    wo.serve(3, 2)
    wo.serve(0, 3)
    attend_pair(6)
    wo.serve(2, 3)
    wo.cross(0, 2)
    wo.cross(3, 1)
    attend_pair(7)
    wo.serve(1, 3)
    wo.serve(3, 3)
    wo.cross(2, 2)
    kvw_cross.wait_send()
    for item in (*kvw_lines, wq):
        item.drain()
    whole = att_buf.at[pl.ds(0, groups)]
    remote(whole, whole, att_send, att_recv, {"blk": p.across + core}).wait_recv()

    def out_copy(k, j, here):
        return remote(out_buf.at[k, j], update_buf.at[y, k], out_send, out_recv.at[y, k],
                      {"blk": chip * 2 + j if here else p.across + j})

    order = [wo.piece(unit, group) for group in (p.group, 1 - p.group) for unit in range(pieces // 2)]
    for i, k in enumerate(order):
        if i == 1:
            wo.cross(1, 2)
            wo.cross(3, 2)
            wo.cross(0, depth - 1)
            wo.cross(2, depth - 1)
        if i == 2:
            wo.cross(1, depth - 1)
            wo.cross(3, depth - 1)
        wo.settle(k)
        total = None
        for c in range(chips):
            product = jnp.dot(att_buf[c], wo_buf[k, c * 2 * rows_each : (c + 1) * 2 * rows_each, :], preferred_element_type=jnp.float32)
            total = product if total is None else total + product
        out_buf[k] = total.astype(jnp.bfloat16).reshape(2, cap, part)

        @pl.when(home_here)
        def _():
            update_buf[y, k] = out_buf[k, core]
            out_copy(k, 1 - core, True).start()

        @pl.when(away)
        def _():
            for j in range(2):
                out_copy(k, j, False).start()

    rows = final_ref[...].astype(jnp.float32)
    gate = jax.nn.sigmoid(jnp.sum(rows * router_ref[...].astype(jnp.float32).reshape(1, width), axis=1, keepdims=True))

    at_slot = lax.broadcasted_iota(jnp.int32, (tokens, cap), 0) == jnp.where(slot < count_ref[...], idx_ref[...], -1)
    put = at_slot.astype(jnp.float32)
    touched = jnp.max(put, axis=1, keepdims=True) > 0.0
    put = put.astype(jnp.bfloat16)

    def spot_of(h, k):
        return pl.ds(pl.multiple_of(h * half + k * part, part), part)

    def placed_copy(h, k):
        cols = spot_of(h, k)
        return pltpu.make_async_copy(placed_buf.at[:, cols], out_ref.at[:, cols], placed_sem)

    def update_wait(h, k):
        remote(out_buf.at[k, 0], update_buf.at[h, k], out_send, out_recv.at[h, k], {"blk": p.across}).wait_recv()

    for i, k in enumerate(order):
        update_wait(1 - y, k)

        @pl.when(away)
        def _():
            update_wait(y, k)

        for h in range(2):
            cols = spot_of(h, k)
            done = (final_ref[:, cols].astype(jnp.float32) + gate * update_buf[h, k].astype(jnp.float32)).astype(jnp.bfloat16)
            placed = jnp.dot(put, done, preferred_element_type=jnp.float32)
            old = hidden_buf[:, cols].astype(jnp.float32)
            placed_buf[:, cols] = jnp.where(touched, placed, old).astype(jnp.bfloat16)
            placed_copy(h, k).start()

    for item in (kv, metas, wo):
        item.drain()
    remote(whole, whole, att_send, att_recv, {"blk": p.across + core}).wait_send()
    rows_copy(1, core).wait_send()
    meta_copy(1, core).wait_send()

    def out_sent(homes):
        some = out_buf.at[:, pl.ds(0, homes)]
        remote(some, some, out_send, out_recv.at[0, 0], {"blk": p.across}).wait_send()

    @pl.when(home_here)
    def _():
        out_sent(1)

    @pl.when(away)
    def _():
        rows_copy(0, core).wait_send()
        meta_copy(0, core).wait_send()
        out_sent(2)

    pltpu.make_async_copy(placed_buf, out_ref, placed_sem).wait()


def layer(n, keep, hidden, kept_idx, kept_count, router, norm_gain, qk_gain, query_weight, key_weight,
          value_weight, out_weight):
    tokens, width = hidden.shape
    cap = kept_idx.shape[1]
    pieces = 4
    lanes, chips, depth = 2 * HEAD, n // 2, n // 4
    half, slots = width // 2, 2 * cap
    part = half // pieces
    rows_each = query_weight.shape[0]
    half_size = HEAD // 2
    rates = rope_base ** (-(np.arange(half_size) * 2.0 / HEAD))
    rates = np.tile(rates, lanes // half_size)[None, :].astype(np.float32)
    dma = pltpu.SemaphoreType.DMA
    small = [
        kept_idx, kept_count.reshape(1, 1), norm_gain.reshape(1, width), router, key_weight, value_weight, qk_gain,
        jnp.asarray(rates),
    ]
    return pl.pallas_call(
        functools.partial(layer_kernel, n, pieces),
        out_shape=jax.ShapeDtypeStruct((tokens, width), jnp.bfloat16),
        in_specs=[HBM] * 11,
        out_specs=ANY,
        scratch_shapes=[pltpu.VMEM(a.shape, a.dtype) for a in small]
        + [
            dma((len(small),)),
            pltpu.VMEM((cap, width), jnp.bfloat16),
            pltpu.VMEM((tokens, width), jnp.bfloat16),
            dma(()),
            pltpu.VMEM((cap, width), jnp.bfloat16),
            pltpu.VMEM((8, cap), jnp.int32),
            pltpu.VMEM((n, 8, cap), jnp.int32),
            pltpu.VMEM((2, cap, width), jnp.bfloat16),
            pltpu.VMEM((2, rows_each, lanes), jnp.bfloat16),
            pltpu.VMEM((width, lanes), jnp.bfloat16),
            pltpu.VMEM((pieces, width, part), jnp.bfloat16),
            pltpu.VMEM((pieces, width, part), jnp.bfloat16),
            pltpu.VMEM((half // HEAD, slots, lanes), jnp.bfloat16),
            pltpu.VMEM((slots, lanes), jnp.bfloat16),
            pltpu.VMEM((n * cap, lanes), jnp.bfloat16),
            pltpu.VMEM((keep, lanes), jnp.bfloat16),
            pltpu.VMEM((slots, keep), jnp.float32),
            pltpu.VMEM((chips, slots, width // chips), jnp.bfloat16),
            pltpu.VMEM((pieces, 2, cap, part), jnp.bfloat16),
            pltpu.VMEM((2, pieces, cap, part), jnp.bfloat16),
            pltpu.VMEM((slots, lanes), jnp.float32),
            pltpu.VMEM((slots, lanes), jnp.float32),
            dma((2,)), dma((2,)), dma((2,)), dma((2,)),
            dma(()), dma(()), dma(()), dma((2, pieces)),
            dma(()), dma(()), pltpu.VMEM((tokens, width), jnp.bfloat16),
        ]
        + [dma((2,))]
        + Line.semaphores(depth, 4)
        + Shared.semaphores(depth, pieces, 2),
        compiler_params=pltpu.CompilerParams(collective_id=1, has_side_effects=True),
    )(hidden, query_weight, out_weight, *small)


def body(
    n,
    hidden,
    kept_idx,
    kept_count,
    router,
    norm_gain,
    qk_gain,
    query_weight,
    key_weight,
    value_weight,
    out_weight,
):
    tokens = hidden.shape[0]
    cap = kept_idx.shape[1]
    keep = n * (tokens * KEEP_DEV // TOK_DEV)
    return layer(
        n, keep, hidden, kept_idx, kept_count, router, norm_gain, qk_gain, query_weight, key_weight,
        value_weight, out_weight,
    )


def attend(query_heads, query_ranks, key_block, value_block, key_ranks, state):
    prev_top, prev_total, prev_acc = state
    length = key_block.shape[0]
    keys_split = key_block.reshape(length, KV_HEADS, HEAD)
    values_split = value_block.reshape(length, KV_HEADS, HEAD)
    scores = jnp.einsum(
        "agch,bgh->gcab", query_heads, keys_split, preferred_element_type=jnp.float32
    ) * (1.0 / math.sqrt(HEAD))
    allowed = key_ranks[None, :] <= query_ranks[:, None]
    masked = jnp.where(allowed, scores, -1e30)
    new_top = jnp.maximum(prev_top, jnp.max(masked, axis=-1))
    weights = jnp.where(allowed, jnp.exp(masked - new_top[..., None]), 0.0)
    factor = jnp.exp(prev_top - new_top)
    new_total = prev_total * factor + jnp.sum(weights, axis=-1)
    new_acc = prev_acc * factor[..., None] + jnp.einsum(
        "gcab,bgh->gcah",
        weights.astype(jnp.bfloat16),
        values_split,
        preferred_element_type=jnp.float32,
    )
    return (new_top, new_total, new_acc)


def make_fold(query_heads, query_ranks, rank_of, state, pieces):
    key_piece, value_piece = pieces
    length = key_piece.shape[0]

    def inner(block_turn, inner_state):
        block_start = block_turn * 512
        key_block = lax.dynamic_slice_in_dim(key_piece, block_start, 512, 0)
        value_block = lax.dynamic_slice_in_dim(value_piece, block_start, 512, 0)
        key_ranks = rank_of(block_start + jnp.arange(512, dtype=jnp.int32))
        return attend(query_heads, query_ranks, key_block, value_block, key_ranks, inner_state)

    return lax.fori_loop(0, length // 512, inner, state)


def wide_body(
    hidden,
    kept_idx,
    kept_count,
    router,
    norm_gain,
    qk_gain,
    query_weight,
    key_weight,
    value_weight,
    out_weight,
):
    shard_count = lax.axis_size("blk")
    device = lax.axis_index("blk")
    width = hidden.shape[1]
    all_lists, all_counts = (
        lax.all_gather(kept_idx, "blk", axis=0, tiled=True),
        lax.all_gather(kept_count, "blk", axis=0, tiled=True),
    )
    starts = jnp.cumsum(all_counts) - all_counts
    own_start = starts[device]
    own_count = all_counts[device]
    list_slots = jnp.arange(CAP, dtype=jnp.int32)
    is_valid = list_slots < own_count
    token_rows = hidden[kept_idx[0]]
    gate_value = jax.nn.sigmoid(jnp.dot(token_rows, router, preferred_element_type=jnp.float32))
    slot_count = (CAP + shard_count - 1) // shard_count
    outgoing = jnp.where(is_valid[:, None], token_rows, jnp.zeros_like(token_rows))
    outgoing = jnp.roll(outgoing.reshape(slot_count, shard_count, width), own_start, axis=1)
    incoming = lax.all_to_all(outgoing, "blk", split_axis=1, concat_axis=1, tiled=True)
    query_ranks = device + jnp.arange(KEEP_DEV, dtype=jnp.int32) * shard_count
    source_ends = starts + all_counts
    source = jnp.sum((source_ends[None, :] <= query_ranks[:, None]).astype(jnp.int32), axis=1)
    within = query_ranks - starts[source]
    flat_index = within // shard_count * shard_count + source
    kept_rows = incoming.reshape(slot_count * shard_count, width)[flat_index]
    positions = source * TOK_DEV + all_lists[source, within]
    row_total = kept_rows.shape[0]
    normed = rms_scale(kept_rows.astype(jnp.float32), norm_gain).astype(jnp.bfloat16)
    query_cols = Q_HEADS * HEAD
    kv_cols = KV_HEADS * HEAD
    full_query, full_key, full_value, full_out = (
        lax.all_gather(query_weight, "blk", axis=0, tiled=True),
        lax.all_gather(key_weight, "blk", axis=0, tiled=True),
        lax.all_gather(value_weight, "blk", axis=0, tiled=True),
        lax.all_gather(out_weight, "blk", axis=0, tiled=True),
    )
    query_lin = jnp.dot(normed, full_query, preferred_element_type=jnp.float32)
    key_lin = jnp.dot(normed, full_key, preferred_element_type=jnp.float32)
    value_lin = jnp.dot(normed, full_value, preferred_element_type=jnp.float32)
    half_size = HEAD // 2
    rotation_rates = rope_base ** (-(jnp.arange(half_size, dtype=jnp.float32) * 2.0 / HEAD))
    angles = (positions.astype(jnp.float32)[:, None] * rotation_rates[None, :])[:, None, :]
    query_heads = rotate(
        rms_scale(query_lin.reshape(row_total, Q_HEADS, HEAD), qk_gain[0]), angles
    ).astype(jnp.bfloat16)
    key_heads = rotate(
        rms_scale(key_lin.reshape(row_total, KV_HEADS, HEAD), qk_gain[1]), angles
    ).astype(jnp.bfloat16)
    query_heads = query_heads.reshape(row_total, KV_HEADS, Q_HEADS // KV_HEADS, HEAD)
    key_flat = key_heads.reshape(row_total, kv_cols)
    value_flat = value_lin.astype(jnp.bfloat16)
    group_size = Q_HEADS // KV_HEADS
    start_state = (
        jnp.full((KV_HEADS, group_size, row_total), -1e30, jnp.float32),
        jnp.zeros((KV_HEADS, group_size, row_total), jnp.float32),
        jnp.zeros((KV_HEADS, group_size, row_total, HEAD), jnp.float32),
    )

    def strided_rank(slots_seen):
        return slots_seen // KEEP_DEV + slots_seen % KEEP_DEV * shard_count

    final_top, final_total, final_acc = make_fold(
        query_heads,
        query_ranks,
        strided_rank,
        start_state,
        (
            lax.all_gather(key_flat, "blk", axis=0, tiled=True),
            lax.all_gather(value_flat, "blk", axis=0, tiled=True),
        ),
    )
    attended = (
        (final_acc / final_total[..., None])
        .transpose(2, 0, 1, 3)
        .reshape(row_total, query_cols)
        .astype(jnp.bfloat16)
    )
    update = jnp.dot(attended, full_out, preferred_element_type=jnp.float32)
    update = update.astype(jnp.bfloat16)
    slot_grid = (
        jnp.arange(slot_count, dtype=jnp.int32)[:, None] * shard_count
        + jnp.mod(device - starts, shard_count)[None, :]
    )
    back_valid = slot_grid < all_counts[None, :]
    local_place = (starts[None, :] + slot_grid - device) // shard_count
    clipped = jnp.where(back_valid, local_place, 0)
    back_rows = jnp.where(back_valid[..., None], update[clipped], jnp.zeros((), jnp.bfloat16))
    returned = lax.all_to_all(back_rows, "blk", split_axis=1, concat_axis=1, tiled=True)
    returned = jnp.roll(returned, -own_start, axis=1).reshape(slot_count * shard_count, width)
    final = (
        token_rows.astype(jnp.float32) + gate_value[:, None] * returned.astype(jnp.float32)
    ).astype(jnp.bfloat16)
    target = jnp.where(is_valid, kept_idx[0], TOK_DEV)
    return hidden.at[target].set(final, mode="drop")


def solution(mesh):
    placed = (
        P(("groups", "blk"), None),
        P(("groups", "blk"), None),
        P(("groups", "blk")),
        P(),
        P(),
        P(),
        P("blk", None),
        P("blk", None),
        P("blk", None),
        P("blk", None),
    )
    n = mesh.shape["blk"]
    by_heads = n % 4 == 0 and Q_HEADS == 2 * n and mesh.shape["groups"] == KV_HEADS
    step = functools.partial(body, n) if by_heads else wide_body
    return jax.shard_map(
        step, mesh=mesh, in_specs=placed, out_specs=P(("groups", "blk"), None), check_vma=False
    )
```
